32 devices in a mesh: wide: 8 (over z, x), narrow: 4 (over y, core).
Axes of the slice: x: 2, y: 2, z: 4, core: 2. Of those that a mesh axis runs over, the one named last changes fastest.
Arguments:
- tokens: bfloat16 [32, 1024, 1024], P(('wide', 'narrow')), may hold values from -6 to 6
- lengths: int32 [32, 8], P(('wide', 'narrow')), may hold values from 1 to 512, 1024 in all within a row
- cotangent: bfloat16 [32, 1024, 1024], P(('wide', 'narrow')), may hold values from -6 to 6
- mixer_weight: bfloat16 [1024, 3072], P(('wide', 'narrow')), may hold values from -0.1875 to 0.1875
- output_weight: bfloat16 [1024, 1024], P(('wide', 'narrow')), may hold values from -0.75 to 0.75
- expand_weight: bfloat16 [1024, 4096], P(('wide', 'narrow')), may hold values from -0.1875 to 0.1875
- contract_weight: bfloat16 [4096, 1024], P(('wide', 'narrow')), may hold values from -0.09375 to 0.09375
- mixer_bias: float32 [3072], replicated, may hold values from -3 to 3
- output_bias: float32 [1024], replicated, may hold values from -2 to 2
- expand_bias: float32 [4096], replicated, may hold values from -3 to 3
- contract_bias: float32 [1024], replicated, may hold values from -2 to 2
- norm_gains: float32 [2, 1024], replicated, may hold values from 0.5 to 1.5
- norm_shifts: float32 [2, 1024], replicated, may hold values from -2 to 2
- prefix_embed: float32 [10, 1024], replicated, may hold values from -6 to 6
- reparam_in: float32 [1024, 512], replicated, may hold values from -0.1875 to 0.1875
- reparam_in_bias: float32 [512], replicated, may hold values from -3 to 3
- reparam_out: float32 [512, 2048], replicated, may hold values from -0.25 to 0.25
- reparam_out_bias: float32 [2048], replicated, may hold values from -3 to 3
Outputs:
- out_tokens: bfloat16 [32, 1024, 1024], P(('wide', 'narrow'))
- grad_tokens: bfloat16 [32, 1024, 1024], P(('wide', 'narrow'))
- grad_embed: float32 [10, 1024], replicated
- grad_in: float32 [1024, 512], replicated
- grad_in_bias: float32 [512], replicated
- grad_out: float32 [512, 2048], replicated
- grad_out_bias: float32 [2048], replicated
The draws below stay inside these ranges and needn't reach their ends.
Inputs may be any that keep to these rules, and one draw needn't show every extreme that they name: Each row of lengths holds 8 document lengths that sum to 1024; in every row one document has exactly 512 tokens.
All inputs are finite; a program needn't handle non-finite values.
Results may differ from the reference program's by a relative error of at most 0.015.
Values may be sent and summed in bfloat16 or wider, within the bound.
A program may use at most 320 MiB of HBM per device.

```python
import math
import jax
import jax.numpy as jnp
import numpy as np
from jax import lax

HEADS = 16
D = 1024
FF = 4096
PREFIX = 10
REP = 512
LEN = 1024
SEGS = 8
MOST = 512
ROWS = 32


def block_scale(key, shape, split, smallest, top_value):
    loudness, own = 1.0, jax.random.fold_in(key, 6)
    for axis_at, blocks in split:
        steps = jnp.exp(jax.random.uniform(jax.random.fold_in(own, axis_at), (blocks,), jnp.float32, smallest / len(split), top_value / len(split)))
        loudness = loudness * jnp.repeat(steps, shape[axis_at] // blocks).reshape([-1 if axis == axis_at else 1 for axis in range(len(shape))])
    return loudness


def split_up(number_of, total, limit, skew):
    portions = [(1 << 20) // math.isqrt(standing ** skew) + 1 for standing in range(2, number_of + 1)]
    rest, counts = total - limit - (number_of - 1), [1] * (number_of - 1)
    while rest > 0:
        free = [i for i in range(number_of - 1) if counts[i] < limit]
        whole, budget = sum([portions[i] for i in free]), rest
        for i in free:
            more = min(limit - counts[i], max(1, budget * portions[i] // whole), rest)
            counts[i] = counts[i] + more
            rest = rest - more
    return np.array([limit] + counts)


def ragged(rng, number_of, total, most, skew):
    if number_of == 2:
        one = jax.random.randint(rng, (), max(1, total - most), min(most, total - 1) + 1)
        return jnp.stack([one, total - one])
    sizes = jnp.asarray(split_up(number_of, total, most, skew), jnp.int32)
    couples = (number_of - 1) // 2
    donor, sink = sizes[1:1 + 2 * couples:2], sizes[2:2 + 2 * couples:2]
    room = jnp.minimum(donor - 1, most - sink)
    passed = jax.random.randint(jax.random.fold_in(rng, 1), (couples,), 0, 1 << 20) % (room + 1)
    sizes = sizes.at[1:1 + 2 * couples:2].set(donor - passed).at[2:2 + 2 * couples:2].set(sink + passed)
    return sizes[jax.random.permutation(jax.random.fold_in(rng, 2), number_of)]


def normal_values(key, shape, scale, limit, shards=(), kind=jnp.bfloat16):
    values = jax.random.normal(key, shape, jnp.float32) * scale
    if len(shards) > 0:
        values = block_scale(key, shape, shards, -0.22, 0.18) * values
    return jnp.clip(values, min=-limit, max=limit).astype(kind)


def setup_inputs(seed: int = 0) -> dict:
    key_of = jax.random.split(jax.random.key(seed), 19)
    tokens = normal_values(key_of[0], (ROWS, LEN, D), 1.0, 6.0, ((0, 32),))
    lengths = jax.vmap(lambda own: ragged(own, SEGS, LEN, MOST, 2))(jax.random.split(key_of[1], ROWS)).reshape((ROWS, SEGS)).astype(jnp.int32)
    cotangent = normal_values(key_of[2], (ROWS, LEN, D), 1.0, 6.0, ((0, 32),))
    mixer_weight = normal_values(key_of[3], (D, 3 * D), D ** -0.5, 0.1875, ((0, 32),))
    output_weight = normal_values(key_of[4], (D, D), (D // 16) ** -0.5, 0.75, ((0, 32),))
    expand_weight = normal_values(key_of[5], (D, FF), D ** -0.5, 0.1875, ((0, 32),))
    contract_weight = normal_values(key_of[6], (FF, D), FF ** -0.5, 0.09375, ((0, 32),))
    mixer_bias = normal_values(key_of[7], (3 * D,), 0.5, 3.0, (), jnp.float32)
    output_bias = normal_values(key_of[8], (D,), 0.3, 2.0, (), jnp.float32)
    expand_bias = normal_values(key_of[9], (FF,), 0.5, 3.0, (), jnp.float32)
    contract_bias = normal_values(key_of[10], (D,), 0.3, 2.0, (), jnp.float32)
    norm_gains = jnp.clip(1.0 + 0.1 * jax.random.normal(key_of[11], (2, D), jnp.float32), 0.5, 1.5)
    norm_shifts = normal_values(key_of[12], (2, D), 0.3, 2.0, (), jnp.float32)
    prefix_embed = normal_values(key_of[13], (PREFIX, D), 1.0, 6.0, (), jnp.float32)
    reparam_in = normal_values(key_of[14], (D, REP), D ** -0.5, 0.1875, (), jnp.float32)
    reparam_in_bias = normal_values(key_of[15], (REP,), 0.5, 3.0, (), jnp.float32)
    reparam_out = normal_values(key_of[16], (REP, 2 * D), REP ** -0.5, 0.25, (), jnp.float32)
    reparam_out_bias = normal_values(key_of[17], (2 * D,), 0.5, 3.0, (), jnp.float32)
    return {"tokens": tokens, "lengths": lengths, "cotangent": cotangent, "mixer_weight": mixer_weight, "output_weight": output_weight, "expand_weight": expand_weight, "contract_weight": contract_weight, "mixer_bias": mixer_bias, "output_bias": output_bias, "expand_bias": expand_bias, "contract_bias": contract_bias, "norm_gains": norm_gains, "norm_shifts": norm_shifts, "prefix_embed": prefix_embed, "reparam_in": reparam_in, "reparam_in_bias": reparam_in_bias, "reparam_out": reparam_out, "reparam_out_bias": reparam_out_bias}


precise = lax.Precision.HIGHEST

@jax.custom_vjp
def low(v):
    return lax.optimization_barrier(v.astype(jnp.bfloat16)).astype(jnp.float32)

@jax.custom_vjp
def low_back(v):
    return v

def low_keep(v):
    return (low(v), None)

def low_pass(kept, grad):
    return (grad,)

def back_keep(v):
    return (v, None)

def back_low(kept, grad):
    return (low(grad),)
low.defvjp(low_keep, low_pass)
low_back.defvjp(back_keep, back_low)

def norm_layer(values, norm_gain, norm_shift):
    center = values - lax.optimization_barrier(jnp.mean(values, axis=-1, keepdims=True))
    spread = lax.optimization_barrier(jnp.mean(center * center, axis=-1, keepdims=True))
    return center * lax.rsqrt(spread + 1e-05) * norm_gain + norm_shift

def matmul(left_side, right_side):
    return jnp.dot(left_side, right_side, precision=precise)

def segment_ids(lengths_row, length):
    segment_ends = jnp.cumsum(lengths_row)
    places = jnp.arange(length, dtype=jnp.int32)
    return lax.optimization_barrier(jnp.sum((places[:, None] >= segment_ends[None, :]).astype(jnp.int32), axis=1))

def attend_row(mixed_row, segments, prefix_kv):
    length = mixed_row.shape[0]
    model_width = mixed_row.shape[1] // 3
    head_size = model_width // HEADS
    score_scale = head_size ** (-0.5)
    block_rows = min(512, length)
    prefix_count = prefix_kv.shape[0]
    key_heads = mixed_row[:, model_width:2 * model_width].reshape(length, HEADS, head_size)
    value_heads = mixed_row[:, 2 * model_width:].reshape(length, HEADS, head_size)
    pre_keys = prefix_kv[:, :model_width].reshape(prefix_count, HEADS, head_size)
    pre_values = prefix_kv[:, model_width:].reshape(prefix_count, HEADS, head_size)
    all_keys = jnp.concatenate([pre_keys, key_heads], axis=0)
    all_values = jnp.concatenate([pre_values, value_heads], axis=0)
    key_pos = jnp.arange(length, dtype=jnp.int32)

    def one_block(first_row):
        queries = lax.dynamic_slice_in_dim(mixed_row, first_row, block_rows, 0)[:, :model_width]
        queries = queries.reshape(block_rows, HEADS, head_size)
        scores = low_back(jnp.einsum('qhd,khd->hqk', queries, all_keys, precision=precise) * score_scale)
        query_pos = first_row + jnp.arange(block_rows, dtype=jnp.int32)
        query_seg = lax.dynamic_slice_in_dim(segments, first_row, block_rows, 0)
        visible = (query_seg[:, None] == segments[None, :]) & (key_pos[None, :] <= query_pos[:, None])
        visible = jnp.concatenate([jnp.ones((block_rows, prefix_count), dtype=jnp.bool_), visible], axis=1)
        probs = low(jax.nn.softmax(jnp.where(visible[None], scores, -1e+30), axis=-1))
        attended = jnp.einsum('hqk,khd->qhd', probs, all_values, precision=precise)
        return attended.reshape(block_rows, model_width)
    first_rows = jnp.arange(length // block_rows, dtype=jnp.int32) * block_rows
    return lax.map(jax.checkpoint(one_block), first_rows).reshape(length, model_width)

def row_forward(inputs, lengths_row, prefix_kv, frozen):
    full_mixer, full_output, full_expand, full_contract, mixer_bias, output_bias, expand_bias, contract_bias, norm_gains, norm_shifts = frozen
    segments = segment_ids(lengths_row, inputs.shape[0])
    normed_one = low(norm_layer(inputs, norm_gains[0], norm_shifts[0]))
    mixed = low(low_back(matmul(normed_one, full_mixer) + mixer_bias))
    attended = low(low_back(attend_row(mixed, segments, prefix_kv)))
    middle = inputs + low_back(matmul(attended, full_output) + output_bias)
    normed_two = low(norm_layer(middle, norm_gains[1], norm_shifts[1]))
    activated = low(jax.nn.gelu(low_back(matmul(normed_two, full_expand) + expand_bias), approximate=True))
    return middle + low_back(matmul(activated, full_contract) + contract_bias)

def reference(tokens, lengths, cotangent, mixer_weight, output_weight, expand_weight, contract_weight, mixer_bias, output_bias, expand_bias, contract_bias, norm_gains, norm_shifts, prefix_embed, reparam_in, reparam_in_bias, reparam_out, reparam_out_bias):
    frozen = (mixer_weight.astype(jnp.float32), output_weight.astype(jnp.float32), expand_weight.astype(jnp.float32), contract_weight.astype(jnp.float32), mixer_bias, output_bias, expand_bias, contract_bias, norm_gains, norm_shifts)

    def forward(inputs, embed_values, in_weight, in_shift, out_weight, out_shift):
        squashed = jnp.tanh(matmul(embed_values, in_weight) + in_shift)
        prefix_kv = low(matmul(squashed, out_weight) + out_shift)

        def one_row(row_items):
            return row_forward(row_items[0], row_items[1], prefix_kv, frozen)
        return lax.map(jax.checkpoint(one_row), (inputs, lengths))
    inputs = tokens.astype(jnp.float32)
    result, backward = jax.vjp(forward, inputs, prefix_embed, reparam_in, reparam_in_bias, reparam_out, reparam_out_bias)
    grads = backward(cotangent.astype(jnp.float32))
    return (result.astype(jnp.bfloat16), grads[0].astype(jnp.bfloat16), grads[1], grads[2], grads[3], grads[4], grads[5])
```

```python
import functools
from functools import partial

import jax
import jax.numpy as jnp
from jax import lax
from jax.experimental import pallas as pl
from jax.experimental.pallas import tpu as pltpu
from jax.sharding import PartitionSpec as P

MOST = 512


def norm_layer(values, norm_gain, norm_shift):
    center = values - jnp.mean(values, axis=-1, keepdims=True)
    spread = jnp.mean(center * center, axis=-1, keepdims=True)
    return center * lax.rsqrt(spread + 1e-05) * norm_gain + norm_shift


def times_transposed(left_side, right_side):
    return lax.dot_general(
        left_side, right_side, (((1,), (1,)), ((), ())), preferred_element_type=jnp.float32
    )


def reparam(embed_values, in_weight, in_shift, out_weight, out_shift):
    squashed = jnp.tanh(
        jnp.dot(embed_values, in_weight, precision=lax.Precision.HIGHEST) + in_shift
    )
    return jnp.dot(squashed, out_weight, precision=lax.Precision.HIGHEST) + out_shift


BLOCK = 256
PAD = 16
F32, BF16 = jnp.float32, jnp.bfloat16


def dot_nt(a, b):
    return lax.dot_general(a, b, (((1,), (1,)), ((), ())), preferred_element_type=F32)


def dot_nn(a, b):
    return lax.dot_general(a, b, (((1,), (0,)), ((), ())), preferred_element_type=F32)


def start_row(lengths_ref, count, length):
    place = lax.broadcasted_iota(jnp.int32, (1, length), 1)
    start = jnp.zeros((1, length), jnp.int32)
    total = jnp.int32(0)
    for j in range(count):
        total = total + lengths_ref[0, j]
        start = jnp.where(place >= total, total, start)
    return start


def visible(start, first_key, keys, first_query, queries, diagonal):
    key = lax.broadcasted_iota(jnp.int32, (keys, queries), 0) + first_key
    seen = key >= start
    if diagonal:
        query = lax.broadcasted_iota(jnp.int32, (keys, queries), 1) + first_query
        seen = seen & (key <= query)
    return seen


def span(qi, most):
    return max(0, qi - most // BLOCK)


def fwd_pair(q2, k_ref, v_ref, pk, pv, start, prefix, most, o_ref, lse_ref):
    length = q2.shape[0]
    lane = lax.broadcasted_iota(jnp.int32, (1, 128), 1)
    pre_seen = lax.broadcasted_iota(jnp.int32, (PAD, BLOCK), 0) < prefix
    v_t = v_ref[...].T
    pv_t = pv.T
    for qi in range(length // BLOCK):
        rows = slice(qi * BLOCK, (qi + 1) * BLOCK)
        lo = span(qi, most)
        st = start[:, rows]
        halves = []
        for h in range(2):
            qh = jnp.where((lane // 64) == h, q2[rows], jnp.zeros((), BF16))
            s_pre = jnp.where(pre_seen, dot_nt(pk, qh), -1e30)
            peak = jnp.max(s_pre, axis=0, keepdims=True)
            parts = []
            for kj in range(lo, qi + 1):
                s = dot_nt(k_ref[kj * BLOCK:(kj + 1) * BLOCK, :], qh)
                s = jnp.where(visible(st, kj * BLOCK, BLOCK, qi * BLOCK, BLOCK, kj == qi), s, -1e30)
                peak = jnp.maximum(peak, jnp.max(s, axis=0, keepdims=True))
                parts.append(s)
            p = jnp.exp(s_pre - peak)
            total = jnp.sum(p, axis=0, keepdims=True)
            o = dot_nn(pv_t[h * 64:(h + 1) * 64], p.astype(BF16))
            for n, kj in enumerate(range(lo, qi + 1)):
                p = jnp.exp(parts[n] - peak)
                total = total + jnp.sum(p, axis=0, keepdims=True)
                o = o + dot_nn(v_t[h * 64:(h + 1) * 64, kj * BLOCK:(kj + 1) * BLOCK], p.astype(BF16))
            halves.append(o / total)
            lse_ref[h:h + 1, rows] = peak + jnp.log(total)
        o_ref[rows, :] = jnp.concatenate(halves, axis=0).T.astype(BF16)


def fwd_kernel(prefix, most, count, len_ref, q_ref, k_ref, v_ref, pk_ref, pv_ref, o_ref, lse_ref):
    start = start_row(len_ref, count, q_ref.shape[0])
    q2 = q_ref[...] * jnp.asarray(0.125, BF16)
    fwd_pair(q2, k_ref, v_ref, pk_ref[...], pv_ref[...], start, prefix, most, o_ref, lse_ref.at[0])


def attend(mixed, lengths, pre, prefix, most):
    length, width = mixed.shape[0], mixed.shape[1] // 3
    pairs = width // 128
    count = lengths.shape[1]
    col = lambda off: pl.BlockSpec((length, 128), lambda p: (0, p + off))
    pcol = lambda off: pl.BlockSpec((PAD, 128), lambda p: (0, p + off))
    return pl.pallas_call(
        functools.partial(fwd_kernel, prefix, most, count),
        grid=(pairs,),
        in_specs=[pl.BlockSpec(memory_space=pltpu.SMEM), col(0), col(pairs), col(2 * pairs), pcol(0), pcol(pairs)],
        out_specs=[col(0), pl.BlockSpec((1, 2, length), lambda p: (p, 0, 0))],
        out_shape=[jax.ShapeDtypeStruct((length, width), BF16), jax.ShapeDtypeStruct((pairs, 2, length), F32)],
        compiler_params=pltpu.CompilerParams(vmem_limit_bytes=48 << 20),
        name="attend",
    )(lengths, mixed, mixed, mixed, pre, pre)


def bwd_kernel(prefix, most, count, len_ref, q_ref, k_ref, v_ref, pk_ref, pv_ref, do_ref, o_ref, lse_ref,
               dq_ref, dk_ref, dv_ref, dpk_ref, dpv_ref, dk_acc, dv_acc):
    length = q_ref.shape[0]
    start = start_row(len_ref, count, length)
    lane = lax.broadcasted_iota(jnp.int32, (1, 128), 1)
    pre_seen = lax.broadcasted_iota(jnp.int32, (PAD, BLOCK), 0) < prefix
    pk, pv = pk_ref[...], pv_ref[...]
    k_t = k_ref[...].T
    pk_t = pk.T
    head_of = lax.broadcasted_iota(jnp.int32, (8, 128), 0)
    pick = ((lax.broadcasted_iota(jnp.int32, (8, 128), 1) // 64) == head_of).astype(F32).astype(BF16)
    for qi in range(length // BLOCK):
        rows = slice(qi * BLOCK, (qi + 1) * BLOCK)
        lo = span(qi, most)
        st = start[:, rows]
        q2 = q_ref[rows, :] * jnp.asarray(0.125, BF16)
        do2 = do_ref[rows, :]
        prod = do2.astype(F32) * o_ref[rows, :].astype(F32)
        high = prod.astype(BF16)
        low = (prod - high.astype(F32)).astype(BF16)
        delta2 = dot_nt(pick, high) + dot_nt(pick, low)
        halves = []
        for h in range(2):
            mine = (lane // 64) == h
            qh = jnp.where(mine, q2, jnp.zeros((), BF16))
            doh = jnp.where(mine, do2, jnp.zeros((), BF16))
            lse = lse_ref[0, h:h + 1, rows]
            delta = delta2[h:h + 1]
            p = jnp.where(pre_seen, jnp.exp(dot_nt(pk, qh) - lse), 0.0)
            ds = (p * (dot_nt(pv, doh) - delta)).astype(BF16)
            dpk = dot_nn(ds, qh)
            dpv = dot_nn(p.astype(BF16), doh)
            if qi == 0 and h == 0:
                dpk_ref[...], dpv_ref[...] = dpk, dpv
            else:
                dpk_ref[...] += dpk
                dpv_ref[...] += dpv
            dq = dot_nn(pk_t[h * 64:(h + 1) * 64], ds)
            for kj in range(lo, qi + 1):
                keys = slice(kj * BLOCK, (kj + 1) * BLOCK)
                s = dot_nt(k_ref[keys, :], qh)
                p = jnp.exp(s - lse)
                p = jnp.where(visible(st, kj * BLOCK, BLOCK, qi * BLOCK, BLOCK, kj == qi), p, 0.0)
                dp = dot_nt(v_ref[keys, :], doh)
                ds = (p * (dp - delta)).astype(BF16)
                dv = dot_nn(p.astype(BF16), doh)
                dk = dot_nn(ds, qh)
                if kj == qi and h == 0:
                    dv_acc[keys, :], dk_acc[keys, :] = dv, dk
                else:
                    dv_acc[keys, :] += dv
                    dk_acc[keys, :] += dk
                dq = dq + dot_nn(k_t[h * 64:(h + 1) * 64, keys], ds)
            halves.append(dq * 0.125)
        dq_ref[rows, :] = jnp.concatenate(halves, axis=0).T.astype(BF16)
    dk_ref[...] = dk_acc[...].astype(BF16)
    dv_ref[...] = dv_acc[...].astype(BF16)


def attend_back(mixed, lengths, pre, grad, attended, lse, prefix, most):
    length, width = grad.shape
    pairs = width // 128
    count = lengths.shape[1]
    col = lambda off: pl.BlockSpec((length, 128), lambda p: (0, p + off))
    pcol = lambda off: pl.BlockSpec((PAD, 128), lambda p: (0, p + off))
    return pl.pallas_call(
        functools.partial(bwd_kernel, prefix, most, count),
        grid=(pairs,),
        in_specs=[pl.BlockSpec(memory_space=pltpu.SMEM), col(0), col(pairs), col(2 * pairs), pcol(0), pcol(pairs),
                  col(0), col(0), pl.BlockSpec((1, 2, length), lambda p: (p, 0, 0))],
        out_specs=[col(0), col(0), col(0), pcol(0), pcol(0)],
        out_shape=[jax.ShapeDtypeStruct((length, width), BF16)] * 3 + [jax.ShapeDtypeStruct((PAD, width), F32)] * 2,
        scratch_shapes=[pltpu.VMEM((length, 128), F32)] * 2,
        compiler_params=pltpu.CompilerParams(vmem_limit_bytes=48 << 20),
        name="attend_back",
    )(lengths, mixed, mixed, mixed, pre, pre, grad, attended, lse)


def shards(
    tokens,
    lengths,
    cotangent,
    mixer_weight,
    output_weight,
    expand_weight,
    contract_weight,
    mixer_bias,
    output_bias,
    expand_bias,
    contract_bias,
    norm_gains,
    norm_shifts,
    prefix_embed,
    reparam_in,
    reparam_in_bias,
    reparam_out,
    reparam_out_bias,
):
    row_count, length, model_width = tokens.shape
    total_rows = row_count * length
    full_mixer, full_output, full_expand, full_contract = (
        lax.all_gather(mixer_weight, ("wide", "narrow"), axis=0, tiled=True),
        lax.all_gather(output_weight, ("wide", "narrow"), axis=0, tiled=True),
        lax.all_gather(expand_weight, ("wide", "narrow"), axis=0, tiled=True),
        lax.all_gather(contract_weight, ("wide", "narrow"), axis=0, tiled=True),
    )
    prefix_kv, reparam_back = jax.vjp(
        reparam, prefix_embed, reparam_in, reparam_in_bias, reparam_out, reparam_out_bias
    )
    prefix_low = prefix_kv.astype(jnp.bfloat16)
    inputs = tokens.reshape(total_rows, model_width).astype(jnp.float32)
    normed_one, norm_one_back = jax.vjp(
        lambda values: norm_layer(values, norm_gains[0], norm_shifts[0]), inputs
    )
    mixed = (
        jnp.dot(normed_one.astype(jnp.bfloat16), full_mixer, preferred_element_type=jnp.float32)
        + mixer_bias
    )
    mixed_low = mixed.astype(jnp.bfloat16)
    prefix_count = prefix_low.shape[0]
    pre = jnp.pad(prefix_low, ((0, PAD - prefix_count), (0, 0)))
    row_of = lambda array, row: array[row * length : (row + 1) * length]
    forward = [
        attend(row_of(mixed_low, row), lengths[row : row + 1], pre, prefix_count, MOST)
        for row in range(row_count)
    ]
    attended = jnp.concatenate([item[0] for item in forward], axis=0)
    middle = inputs + (
        jnp.dot(attended, full_output, preferred_element_type=jnp.float32) + output_bias
    )
    normed_two, norm_two_back = jax.vjp(
        lambda values: norm_layer(values, norm_gains[1], norm_shifts[1]), middle
    )
    expanded = (
        jnp.dot(normed_two.astype(jnp.bfloat16), full_expand, preferred_element_type=jnp.float32)
        + expand_bias
    )
    activated, gelu_back = jax.vjp(partial(jax.nn.gelu, approximate=True), expanded)
    result = middle + (
        jnp.dot(activated.astype(jnp.bfloat16), full_contract, preferred_element_type=jnp.float32)
        + contract_bias
    )
    out_tokens = result.astype(jnp.bfloat16).reshape(row_count, length, model_width)
    back_mixer, back_output, back_expand, back_contract = (
        lax.all_gather(mixer_weight, ("wide", "narrow"), axis=0, tiled=True),
        lax.all_gather(output_weight, ("wide", "narrow"), axis=0, tiled=True),
        lax.all_gather(expand_weight, ("wide", "narrow"), axis=0, tiled=True),
        lax.all_gather(contract_weight, ("wide", "narrow"), axis=0, tiled=True),
    )
    grad_result = cotangent.reshape(total_rows, model_width)
    grad_activated = times_transposed(grad_result, back_contract)
    grad_expanded = gelu_back(grad_activated)[0].astype(jnp.bfloat16)
    grad_normed_two = times_transposed(grad_expanded, back_expand)
    grad_middle = grad_result.astype(jnp.float32) + norm_two_back(grad_normed_two)[0]
    grad_attended = times_transposed(grad_middle.astype(jnp.bfloat16), back_output).astype(
        jnp.bfloat16
    )
    back = [
        attend_back(
            row_of(mixed_low, row), lengths[row : row + 1], pre, row_of(grad_attended, row),
            forward[row][0], forward[row][1], prefix_count, MOST,
        )
        for row in range(row_count)
    ]
    grad_mixed = jnp.concatenate(
        [jnp.concatenate([item[part] for item in back], axis=0) for part in range(3)], axis=1
    )
    grad_prefix = jnp.concatenate(
        [sum(item[part] for item in back)[:prefix_count] for part in (3, 4)], axis=1
    )
    grad_prefix = lax.psum(grad_prefix, ("wide", "narrow"))
    grad_normed_one = times_transposed(grad_mixed, back_mixer)
    grad_inputs = (grad_middle + norm_one_back(grad_normed_one)[0]).astype(jnp.bfloat16)
    grad_inputs = grad_inputs.reshape(row_count, length, model_width)
    grad_embed, grad_in, grad_in_bias, grad_out, grad_out_bias = reparam_back(grad_prefix)
    return (out_tokens, grad_inputs, grad_embed, grad_in, grad_in_bias, grad_out, grad_out_bias)


def solution(mesh):
    return jax.shard_map(
        shards,
        mesh=mesh,
        in_specs=(
            P(("wide", "narrow"), None, None),
            P(("wide", "narrow"), None),
            P(("wide", "narrow"), None, None),
            P(("wide", "narrow"), None),
            P(("wide", "narrow"), None),
            P(("wide", "narrow"), None),
            P(("wide", "narrow"), None),
            P(),
            P(),
            P(),
            P(),
            P(),
            P(),
            P(),
            P(),
            P(),
            P(),
            P(),
        ),
        out_specs=(
            P(("wide", "narrow"), None, None),
            P(("wide", "narrow"), None, None),
            P(),
            P(),
            P(),
            P(),
            P(),
        ),
        check_vma=False,
    )
```

```python
import functools
import math

import jax
import jax.numpy as jnp
from jax import lax
from jax.experimental import pallas as pl
from jax.experimental.pallas import tpu as pltpu
from jax.sharding import PartitionSpec as P

MOST = 512


def norm_layer(values, norm_gain, norm_shift):
    center = values - jnp.mean(values, axis=-1, keepdims=True)
    spread = jnp.mean(center * center, axis=-1, keepdims=True)
    return center * lax.rsqrt(spread + 1e-05) * norm_gain + norm_shift


def times_transposed(left_side, right_side):
    return lax.dot_general(
        left_side, right_side, (((1,), (1,)), ((), ())), preferred_element_type=jnp.float32
    )


def reparam(embed_values, in_weight, in_shift, out_weight, out_shift):
    squashed = jnp.tanh(
        jnp.dot(embed_values, in_weight, precision=lax.Precision.HIGHEST) + in_shift
    )
    return jnp.dot(squashed, out_weight, precision=lax.Precision.HIGHEST) + out_shift


BLOCK = 256
PAD = 16
F32, BF16 = jnp.float32, jnp.bfloat16


def dot_nt(a, b):
    return lax.dot_general(a, b, (((1,), (1,)), ((), ())), preferred_element_type=F32)


def dot_nn(a, b):
    return lax.dot_general(a, b, (((1,), (0,)), ((), ())), preferred_element_type=F32)


def start_row(lengths_ref, count, length):
    place = lax.broadcasted_iota(jnp.int32, (1, length), 1)
    start = jnp.zeros((1, length), jnp.int32)
    total = jnp.int32(0)
    for j in range(count):
        total = total + lengths_ref[0, j]
        start = jnp.where(place >= total, total, start)
    return start


def visible(start, first_key, keys, first_query, queries, diagonal):
    key = lax.broadcasted_iota(jnp.int32, (keys, queries), 0) + first_key
    seen = key >= start
    if diagonal:
        query = lax.broadcasted_iota(jnp.int32, (keys, queries), 1) + first_query
        seen = seen & (key <= query)
    return seen


def span(qi, most):
    return max(0, qi - most // BLOCK)


def fwd_pair(q2, k_ref, v_ref, pk, pv, start, prefix, most, o_ref, lse_ref):
    length = q2.shape[0]
    lane = lax.broadcasted_iota(jnp.int32, (1, 128), 1)
    pre_seen = lax.broadcasted_iota(jnp.int32, (PAD, BLOCK), 0) < prefix
    v_t = v_ref[...].T
    pv_t = pv.T
    for qi in range(length // BLOCK):
        rows = slice(qi * BLOCK, (qi + 1) * BLOCK)
        lo = span(qi, most)
        st = start[:, rows]
        halves = []
        for h in range(2):
            qh = jnp.where((lane // 64) == h, q2[rows], jnp.zeros((), BF16))
            s_pre = jnp.where(pre_seen, dot_nt(pk, qh), -1e30)
            peak = jnp.max(s_pre, axis=0, keepdims=True)
            parts = []
            for kj in range(lo, qi + 1):
                s = dot_nt(k_ref[kj * BLOCK:(kj + 1) * BLOCK, :], qh)
                s = jnp.where(visible(st, kj * BLOCK, BLOCK, qi * BLOCK, BLOCK, kj == qi), s, -1e30)
                peak = jnp.maximum(peak, jnp.max(s, axis=0, keepdims=True))
                parts.append(s)
            p = jnp.exp(s_pre - peak)
            total = jnp.sum(p, axis=0, keepdims=True)
            o = dot_nn(pv_t[h * 64:(h + 1) * 64], p.astype(BF16))
            for n, kj in enumerate(range(lo, qi + 1)):
                p = jnp.exp(parts[n] - peak)
                total = total + jnp.sum(p, axis=0, keepdims=True)
                o = o + dot_nn(v_t[h * 64:(h + 1) * 64, kj * BLOCK:(kj + 1) * BLOCK], p.astype(BF16))
            halves.append(o / total)
            lse_ref[h:h + 1, rows] = peak + jnp.log(total)
        o_ref[rows, :] = jnp.concatenate(halves, axis=0).T.astype(BF16)


def fwd_kernel(prefix, most, count, len_ref, q_ref, k_ref, v_ref, pk_ref, pv_ref, o_ref, lse_ref):
    start = start_row(len_ref, count, q_ref.shape[0])
    q2 = q_ref[...] * jnp.asarray(0.125, BF16)
    fwd_pair(q2, k_ref, v_ref, pk_ref[...], pv_ref[...], start, prefix, most, o_ref, lse_ref.at[0])


def attend(mixed, lengths, pre, prefix, most):
    length, width = mixed.shape[0], mixed.shape[1] // 3
    pairs = width // 128
    count = lengths.shape[1]
    col = lambda off: pl.BlockSpec((length, 128), lambda p: (0, p + off))
    pcol = lambda off: pl.BlockSpec((PAD, 128), lambda p: (0, p + off))
    return pl.pallas_call(
        functools.partial(fwd_kernel, prefix, most, count),
        grid=(pairs,),
        in_specs=[pl.BlockSpec(memory_space=pltpu.SMEM), col(0), col(pairs), col(2 * pairs), pcol(0), pcol(pairs)],
        out_specs=[col(0), pl.BlockSpec((1, 2, length), lambda p: (p, 0, 0))],
        out_shape=[jax.ShapeDtypeStruct((length, width), BF16), jax.ShapeDtypeStruct((pairs, 2, length), F32)],
        compiler_params=pltpu.CompilerParams(vmem_limit_bytes=48 << 20),
        name="attend",
    )(lengths, mixed, mixed, mixed, pre, pre)


def bwd_kernel(prefix, most, count, len_ref, q_ref, k_ref, v_ref, pk_ref, pv_ref, do_ref, o_ref, lse_ref,
               dq_ref, dk_ref, dv_ref, dpk_ref, dpv_ref, dk_acc, dv_acc):
    length = q_ref.shape[0]
    start = start_row(len_ref, count, length)
    lane = lax.broadcasted_iota(jnp.int32, (1, 128), 1)
    pre_seen = lax.broadcasted_iota(jnp.int32, (PAD, BLOCK), 0) < prefix
    pk, pv = pk_ref[...], pv_ref[...]
    k_t = k_ref[...].T
    pk_t = pk.T
    head_of = lax.broadcasted_iota(jnp.int32, (8, 128), 0)
    pick = ((lax.broadcasted_iota(jnp.int32, (8, 128), 1) // 64) == head_of).astype(F32).astype(BF16)
    for qi in range(length // BLOCK):
        rows = slice(qi * BLOCK, (qi + 1) * BLOCK)
        lo = span(qi, most)
        st = start[:, rows]
        q2 = q_ref[rows, :] * jnp.asarray(0.125, BF16)
        do2 = do_ref[rows, :]
        prod = do2.astype(F32) * o_ref[rows, :].astype(F32)
        high = prod.astype(BF16)
        low = (prod - high.astype(F32)).astype(BF16)
        delta2 = dot_nt(pick, high) + dot_nt(pick, low)
        halves = []
        for h in range(2):
            mine = (lane // 64) == h
            qh = jnp.where(mine, q2, jnp.zeros((), BF16))
            doh = jnp.where(mine, do2, jnp.zeros((), BF16))
            lse = lse_ref[0, h:h + 1, rows]
            delta = delta2[h:h + 1]
            p = jnp.where(pre_seen, jnp.exp(dot_nt(pk, qh) - lse), 0.0)
            ds = (p * (dot_nt(pv, doh) - delta)).astype(BF16)
            dpk = dot_nn(ds, qh)
            dpv = dot_nn(p.astype(BF16), doh)
            if qi == 0 and h == 0:
                dpk_ref[...], dpv_ref[...] = dpk, dpv
            else:
                dpk_ref[...] += dpk
                dpv_ref[...] += dpv
            dq = dot_nn(pk_t[h * 64:(h + 1) * 64], ds)
            for kj in range(lo, qi + 1):
                keys = slice(kj * BLOCK, (kj + 1) * BLOCK)
                s = dot_nt(k_ref[keys, :], qh)
                p = jnp.exp(s - lse)
                p = jnp.where(visible(st, kj * BLOCK, BLOCK, qi * BLOCK, BLOCK, kj == qi), p, 0.0)
                dp = dot_nt(v_ref[keys, :], doh)
                ds = (p * (dp - delta)).astype(BF16)
                dv = dot_nn(p.astype(BF16), doh)
                dk = dot_nn(ds, qh)
                if kj == qi and h == 0:
                    dv_acc[keys, :], dk_acc[keys, :] = dv, dk
                else:
                    dv_acc[keys, :] += dv
                    dk_acc[keys, :] += dk
                dq = dq + dot_nn(k_t[h * 64:(h + 1) * 64, keys], ds)
            halves.append(dq * 0.125)
        dq_ref[rows, :] = jnp.concatenate(halves, axis=0).T.astype(BF16)
    dk_ref[...] = dk_acc[...].astype(BF16)
    dv_ref[...] = dv_acc[...].astype(BF16)


def attend_back(mixed, lengths, pre, grad, attended, lse, prefix, most):
    length, width = grad.shape
    pairs = width // 128
    count = lengths.shape[1]
    col = lambda off: pl.BlockSpec((length, 128), lambda p: (0, p + off))
    pcol = lambda off: pl.BlockSpec((PAD, 128), lambda p: (0, p + off))
    return pl.pallas_call(
        functools.partial(bwd_kernel, prefix, most, count),
        grid=(pairs,),
        in_specs=[pl.BlockSpec(memory_space=pltpu.SMEM), col(0), col(pairs), col(2 * pairs), pcol(0), pcol(pairs),
                  col(0), col(0), pl.BlockSpec((1, 2, length), lambda p: (p, 0, 0))],
        out_specs=[col(0), col(0), col(0), pcol(0), pcol(0)],
        out_shape=[jax.ShapeDtypeStruct((length, width), BF16)] * 3 + [jax.ShapeDtypeStruct((PAD, width), F32)] * 2,
        scratch_shapes=[pltpu.VMEM((length, 128), F32)] * 2,
        compiler_params=pltpu.CompilerParams(vmem_limit_bytes=48 << 20),
        name="attend_back",
    )(lengths, mixed, mixed, mixed, pre, pre, grad, attended, lse)


MESH = pl.DeviceIdType.MESH
CHUNKS = 8
LAG = 2
AHEAD = 3
TILE = 256


def grid_dims(mesh_shape):
    wide, narrow = mesh_shape["wide"], mesh_shape["narrow"]
    return (wide // 2, 2, narrow // 2, 2)


class Gather:
    def __init__(self, dims, families):
        self.dims = dims
        wide, narrow = lax.axis_index("wide"), lax.axis_index("narrow")
        self.at = (wide // dims[1], lax.rem(wide, dims[1]), narrow // dims[3], lax.rem(narrow, dims[3]))
        self.families = families

    def device(self, dim, index):
        at = list(self.at)
        at[dim] = index
        return (at[0] * self.dims[1] + at[1], at[2] * self.dims[3] + at[3])

    def greet(self):
        barrier = pltpu.get_barrier_semaphore()
        count = 0
        for dim, size in enumerate(self.dims):
            for step in range(1, size):
                peer = self.device(dim, lax.rem(self.at[dim] + step, size))
                pl.semaphore_signal(barrier, inc=1, device_id=peer, device_id_type=MESH)
                count += 1
        pl.semaphore_wait(barrier, count)

    def view(self, family, j, stage, index):
        _, target, order, _, _, _ = family
        done, dim = order[:stage], order[stage]
        return target.at[
            (j,) + tuple(slice(None) if d in done else (index if d == dim else self.at[d]) for d in range(4))
        ]

    def own(self, family, j):
        source, target, _, _, _, own = family
        return pltpu.make_async_copy(source.at[j], target.at[(j,) + self.at], own.at[j])

    def start(self, j, stage):
        for family in self.families:
            source, _, order, send, recv, _ = family
            dim = order[stage]
            size = self.dims[dim]
            if stage == 0:
                self.own(family, j).start()
            mine = self.view(family, j, stage, self.at[dim])
            for step in range(1, size):
                pltpu.make_async_remote_copy(
                    src_ref=source.at[j] if stage == 0 else mine,
                    dst_ref=mine,
                    send_sem=send.at[j, stage],
                    recv_sem=recv.at[j, stage],
                    device_id=self.device(dim, lax.rem(self.at[dim] + step, size)),
                    device_id_type=MESH,
                ).start()

    def whole(self, family, j, stage):
        _, _, order, send, recv, _ = family
        size = self.dims[order[stage]]
        part = self.view(family, j, stage, pl.ds(0, size - 1))
        return pltpu.make_async_remote_copy(
            src_ref=part, dst_ref=part, send_sem=send.at[j, stage], recv_sem=recv.at[j, stage],
            device_id=self.device(order[stage], lax.rem(self.at[order[stage]] + 1, size)), device_id_type=MESH,
        )

    def arrive(self, j, stage):
        for family in self.families:
            if stage == 0:
                self.own(family, j).wait()
            self.whole(family, j, stage).wait_recv()

    def finish(self, count):
        @pl.loop(0, count)
        def _(j):
            for family in self.families:
                for stage in range(4):
                    self.whole(family, j, stage).wait_send()

    def tick(self, t, count):
        @pl.when(t + AHEAD < count)
        def _():
            self.start(t + AHEAD, 0)

        for stage in (2, 1, 0):
            j = t - LAG * stage

            @pl.when((j >= 0) & (j < count))
            def _():
                self.arrive(j, stage)
                self.start(j, stage + 1)

        j = t - LAG * 3

        @pl.when((j >= 0) & (j < count))
        def _():
            self.arrive(j, 3)


XY, YX = (0, 1, 2, 3), (0, 2, 1, 3)


def norm_parts(values):
    center = values - jnp.mean(values, axis=-1, keepdims=True)
    rate = lax.rsqrt(jnp.mean(center * center, axis=-1, keepdims=True) + 1e-05)
    return center * rate, rate


def norm_back(hat, rate, grad, gain):
    inner = grad * gain
    return rate * (
        inner - jnp.mean(inner, axis=-1, keepdims=True) - hat * jnp.mean(inner * hat, axis=-1, keepdims=True)
    )


ROOT = math.sqrt(2.0 / math.pi)


def gelu_both(v):
    square = v * v
    th = jnp.tanh(ROOT * v * (1.0 + 0.044715 * square))
    half = 0.5 * (1.0 + th)
    slope = half + 0.5 * v * (1.0 - th * th) * (ROOT * (1.0 + 3 * 0.044715 * square))
    return v * half, slope


def ff_kernel(dims, x_hbm, cot_hbm, att_hbm, wo_hbm, e_hbm, c_hbm, bo_ref, be_ref, bc_ref, gain_ref, shift_ref,
              out_hbm, gm_hbm, ga_hbm,
              ew, cw, x, cot, att, wo, n2, mid, acc, gacc,
              e_send, e_recv, e_own, c_send, c_recv, c_own, in_sems, out_sems):
    length, width = x.shape
    count = e_hbm.shape[0]
    gather = Gather(dims, [(e_hbm, ew, XY, e_send, e_recv, e_own), (c_hbm, cw, YX, c_send, c_recv, c_own)])
    loads = [
        pltpu.make_async_copy(src, dst, in_sems.at[n])
        for n, (src, dst) in enumerate(((x_hbm, x), (att_hbm, att), (wo_hbm, wo), (cot_hbm, cot)))
    ]
    for load in loads:
        load.start()
    gather.greet()
    for j in range(min(AHEAD, count)):
        gather.start(j, 0)
    for load in loads:
        load.wait()
    gain, shift = gain_ref[...], shift_ref[...]
    tiles = length // TILE

    def rows_of(i):
        return pl.ds(pl.multiple_of(i * TILE, TILE), TILE)

    def before(i):
        rows = rows_of(i)
        value = x[rows, :].astype(F32) + (dot_nn(att[rows, :], wo[...]) + bo_ref[...])
        mid[rows, :] = value
        hat, _ = norm_parts(value)
        n2[rows, :] = (hat * gain + shift).astype(BF16)
        acc[rows, :] = jnp.zeros((TILE, width), F32)
        gacc[rows, :] = jnp.zeros((TILE, width), F32)

    def chunk(j):
        e = ew.at[j]
        c = cw.at[j]
        bias = be_ref[pl.ds(j, 1), :]

        @pl.loop(0, tiles)
        def _(i):
            rows = rows_of(i)
            ev = e[...].reshape(width, -1)
            cv = c[...].reshape(-1, width)
            active, slope = gelu_both(dot_nn(n2[rows, :], ev) + bias)
            grad = (dot_nt(cot[rows, :], cv) * slope).astype(BF16)
            acc[rows, :] += dot_nn(active.astype(BF16), cv)
            gacc[rows, :] += dot_nt(grad, ev)

    @pl.loop(0, max(count + 3 * LAG, tiles))
    def _(t):
        gather.tick(t, count)

        @pl.when(t < tiles)
        def _():
            before(t)

        j = t - 3 * LAG

        @pl.when((j >= 0) & (j < count))
        def _():
            chunk(j)

    def stores(i):
        rows = rows_of(i)
        return [
            pltpu.make_async_copy(src.at[rows, :], dst.at[rows, :], out_sems.at[n, i])
            for n, (src, dst) in enumerate(((x, out_hbm), (gacc, gm_hbm), (att, ga_hbm)))
        ]

    @pl.loop(0, tiles)
    def _(i):
        rows = rows_of(i)
        value = mid[rows, :]
        x[rows, :] = (value + (acc[rows, :] + bc_ref[...])).astype(BF16)
        hat, rate = norm_parts(value)
        grad = cot[rows, :].astype(F32) + norm_back(hat, rate, gacc[rows, :], gain)
        gacc[rows, :] = grad
        att[rows, :] = dot_nt(grad.astype(BF16), wo[...]).astype(BF16)
        for store in stores(i):
            store.start()

    gather.finish(count)

    @pl.loop(0, tiles)
    def _(i):
        for store in stores(i):
            store.wait()


def feed_forward(dims, x, cot, attended, full_output, e_shard, c_shard, bo, be, bc, gain, shift):
    length, width = x.shape
    chunks = e_shard.shape[0]
    columns = be.shape[1]
    anyspace = pl.BlockSpec(memory_space=pl.ANY)
    vmem = pl.BlockSpec(memory_space=pltpu.VMEM)
    dma = pltpu.SemaphoreType.DMA
    full = lambda kind: pltpu.VMEM((length, width), kind)
    return pl.pallas_call(
        functools.partial(ff_kernel, dims),
        in_specs=[anyspace] * 6 + [vmem] * 5,
        out_specs=[anyspace] * 3,
        out_shape=[jax.ShapeDtypeStruct((length, width), kind) for kind in (BF16, F32, BF16)],
        scratch_shapes=[
            pltpu.VMEM((chunks,) + dims + e_shard.shape[1:], BF16),
            pltpu.VMEM((chunks,) + dims + c_shard.shape[1:], BF16),
            full(BF16), full(BF16), full(BF16), pltpu.VMEM((width, width), BF16),
            full(BF16), full(F32), full(F32), full(F32),
            dma((chunks, 4)), dma((chunks, 4)), dma((chunks,)),
            dma((chunks, 4)), dma((chunks, 4)), dma((chunks,)),
            dma((4,)), dma((3, length // TILE)),
        ],
        compiler_params=pltpu.CompilerParams(collective_id=1, has_side_effects=True, vmem_limit_bytes=58 << 20),
        name="feed_forward",
    )(x, cot, attended, full_output, e_shard, c_shard, bo, be, bc, gain, shift)


def shards(
    dims,
    tokens,
    lengths,
    cotangent,
    mixer_weight,
    output_weight,
    expand_weight,
    contract_weight,
    mixer_bias,
    output_bias,
    expand_bias,
    contract_bias,
    norm_gains,
    norm_shifts,
    prefix_embed,
    reparam_in,
    reparam_in_bias,
    reparam_out,
    reparam_out_bias,
):
    row_count, length, model_width = tokens.shape
    total_rows = row_count * length
    full_mixer = lax.all_gather(mixer_weight, ("wide", "narrow"), axis=0, tiled=True)
    full_output = lax.all_gather(output_weight, ("wide", "narrow"), axis=0, tiled=True)
    devices = math.prod(dims)
    hidden = expand_weight.shape[1]
    part = hidden // devices // CHUNKS
    by_chunk = lambda array: array.reshape(-1, devices, CHUNKS, part).transpose(2, 0, 1, 3).reshape(CHUNKS, -1, devices * part)
    expand_parts = by_chunk(expand_weight)
    expand_bias_parts = by_chunk(expand_bias)[:, 0]
    contract_parts = contract_weight.reshape(CHUNKS, part, model_width)
    prefix_kv, reparam_back = jax.vjp(
        reparam, prefix_embed, reparam_in, reparam_in_bias, reparam_out, reparam_out_bias
    )
    prefix_low = prefix_kv.astype(jnp.bfloat16)
    inputs = tokens.reshape(total_rows, model_width).astype(jnp.float32)
    normed_one, norm_one_back = jax.vjp(
        lambda values: norm_layer(values, norm_gains[0], norm_shifts[0]), inputs
    )
    mixed = (
        jnp.dot(normed_one.astype(jnp.bfloat16), full_mixer, preferred_element_type=jnp.float32)
        + mixer_bias
    )
    mixed_low = mixed.astype(jnp.bfloat16)
    prefix_count = prefix_low.shape[0]
    pre = jnp.pad(prefix_low, ((0, PAD - prefix_count), (0, 0)))
    row_of = lambda array, row: array[row * length : (row + 1) * length]
    forward = [
        attend(row_of(mixed_low, row), lengths[row : row + 1], pre, prefix_count, MOST)
        for row in range(row_count)
    ]
    attended = jnp.concatenate([item[0] for item in forward], axis=0)
    as_row = lambda array: array.reshape(1, -1)
    out_tokens, grad_middle, grad_attended = feed_forward(
        dims, tokens.reshape(total_rows, model_width), cotangent.reshape(total_rows, model_width), attended, full_output,
        expand_parts, contract_parts, as_row(output_bias), expand_bias_parts, as_row(contract_bias),
        norm_gains[1:2], norm_shifts[1:2],
    )
    out_tokens = out_tokens.reshape(row_count, length, model_width)
    back = [
        attend_back(
            row_of(mixed_low, row), lengths[row : row + 1], pre, row_of(grad_attended, row),
            forward[row][0], forward[row][1], prefix_count, MOST,
        )
        for row in range(row_count)
    ]
    grad_mixed = jnp.concatenate(
        [jnp.concatenate([item[part] for item in back], axis=0) for part in range(3)], axis=1
    )
    grad_prefix = jnp.concatenate(
        [sum(item[part] for item in back)[:prefix_count] for part in (3, 4)], axis=1
    )
    grad_prefix = lax.psum(grad_prefix, ("wide", "narrow"))
    grad_normed_one = times_transposed(grad_mixed, full_mixer)
    grad_inputs = (grad_middle + norm_one_back(grad_normed_one)[0]).astype(jnp.bfloat16)
    grad_inputs = grad_inputs.reshape(row_count, length, model_width)
    grad_embed, grad_in, grad_in_bias, grad_out, grad_out_bias = reparam_back(grad_prefix)
    return (out_tokens, grad_inputs, grad_embed, grad_in, grad_in_bias, grad_out, grad_out_bias)


def solution(mesh):
    return jax.shard_map(
        functools.partial(shards, grid_dims(mesh.shape)),
        mesh=mesh,
        in_specs=(
            P(("wide", "narrow"), None, None),
            P(("wide", "narrow"), None),
            P(("wide", "narrow"), None, None),
            P(("wide", "narrow"), None),
            P(("wide", "narrow"), None),
            P(("wide", "narrow"), None),
            P(("wide", "narrow"), None),
            P(),
            P(),
            P(),
            P(),
            P(),
            P(),
            P(),
            P(),
            P(),
            P(),
            P(),
        ),
        out_specs=(
            P(("wide", "narrow"), None, None),
            P(("wide", "narrow"), None, None),
            P(),
            P(),
            P(),
            P(),
            P(),
        ),
        check_vma=False,
    )
```

```python
import functools
import math

import jax
import jax.numpy as jnp
from jax import lax
from jax.experimental import pallas as pl
from jax.experimental.pallas import tpu as pltpu
from jax.sharding import PartitionSpec as P

MOST = 512


def norm_layer(values, norm_gain, norm_shift):
    center = values - jnp.mean(values, axis=-1, keepdims=True)
    spread = jnp.mean(center * center, axis=-1, keepdims=True)
    return center * lax.rsqrt(spread + 1e-05) * norm_gain + norm_shift


BLOCK = 256
PAD = 16
F32, BF16 = jnp.float32, jnp.bfloat16


def dot_nt(a, b):
    return lax.dot_general(a, b, (((1,), (1,)), ((), ())), preferred_element_type=F32)


def dot_nn(a, b):
    return lax.dot_general(a, b, (((1,), (0,)), ((), ())), preferred_element_type=F32)


def start_row(lengths_ref, count, length):
    place = lax.broadcasted_iota(jnp.int32, (1, length), 1)
    start = jnp.zeros((1, length), jnp.int32)
    total = jnp.int32(0)
    for j in range(count):
        total = total + lengths_ref[0, j]
        start = jnp.where(place >= total, total, start)
    return start


def visible(start, first_key, keys, first_query, queries, diagonal):
    key = lax.broadcasted_iota(jnp.int32, (keys, queries), 0) + first_key
    seen = key >= start
    if diagonal:
        query = lax.broadcasted_iota(jnp.int32, (keys, queries), 1) + first_query
        seen = seen & (key <= query)
    return seen


def span(qi, most):
    return max(0, qi - most // BLOCK)


def fwd_pair(q2, k_ref, v_ref, pk, pv, start, prefix, most, o_ref, lse_ref):
    length = q2.shape[0]
    lane = lax.broadcasted_iota(jnp.int32, (1, 128), 1)
    pre_seen = lax.broadcasted_iota(jnp.int32, (PAD, BLOCK), 0) < prefix
    v_t = v_ref[...].T
    pv_t = pv.T
    for qi in range(length // BLOCK):
        rows = slice(qi * BLOCK, (qi + 1) * BLOCK)
        lo = span(qi, most)
        st = start[:, rows]
        halves = []
        for h in range(2):
            qh = jnp.where((lane // 64) == h, q2[rows], jnp.zeros((), BF16))
            s_pre = jnp.where(pre_seen, dot_nt(pk, qh), -1e30)
            peak = jnp.max(s_pre, axis=0, keepdims=True)
            parts = []
            for kj in range(lo, qi + 1):
                s = dot_nt(k_ref[kj * BLOCK:(kj + 1) * BLOCK, :], qh)
                s = jnp.where(visible(st, kj * BLOCK, BLOCK, qi * BLOCK, BLOCK, kj == qi), s, -1e30)
                peak = jnp.maximum(peak, jnp.max(s, axis=0, keepdims=True))
                parts.append(s)
            p = jnp.exp(s_pre - peak)
            total = jnp.sum(p, axis=0, keepdims=True)
            o = dot_nn(pv_t[h * 64:(h + 1) * 64], p.astype(BF16))
            for n, kj in enumerate(range(lo, qi + 1)):
                p = jnp.exp(parts[n] - peak)
                total = total + jnp.sum(p, axis=0, keepdims=True)
                o = o + dot_nn(v_t[h * 64:(h + 1) * 64, kj * BLOCK:(kj + 1) * BLOCK], p.astype(BF16))
            halves.append(o / total)
            lse_ref[h:h + 1, rows] = peak + jnp.log(total)
        o_ref[rows, :] = jnp.concatenate(halves, axis=0).T.astype(BF16)


def fwd_kernel(prefix, most, count, len_ref, q_ref, k_ref, v_ref, pk_ref, pv_ref, o_ref, lse_ref):
    start = start_row(len_ref, count, q_ref.shape[0])
    q2 = q_ref[...] * jnp.asarray(0.125, BF16)
    fwd_pair(q2, k_ref, v_ref, pk_ref[...], pv_ref[...], start, prefix, most, o_ref, lse_ref.at[0])


def attend(mixed, lengths, pre, prefix, most):
    length, width = mixed.shape[0], mixed.shape[1] // 3
    pairs = width // 128
    count = lengths.shape[1]
    col = lambda off: pl.BlockSpec((length, 128), lambda p: (0, p + off))
    pcol = lambda off: pl.BlockSpec((PAD, 128), lambda p: (0, p + off))
    return pl.pallas_call(
        functools.partial(fwd_kernel, prefix, most, count),
        grid=(pairs,),
        in_specs=[pl.BlockSpec(memory_space=pltpu.SMEM), col(0), col(pairs), col(2 * pairs), pcol(0), pcol(pairs)],
        out_specs=[col(0), pl.BlockSpec((1, 2, length), lambda p: (p, 0, 0))],
        out_shape=[jax.ShapeDtypeStruct((length, width), BF16), jax.ShapeDtypeStruct((pairs, 2, length), F32)],
        compiler_params=pltpu.CompilerParams(vmem_limit_bytes=48 << 20),
        name="attend",
    )(lengths, mixed, mixed, mixed, pre, pre)


MESH = pl.DeviceIdType.MESH
CHUNKS = 8
LAG = 2
AHEAD = 3
TILE = 256


def grid_dims(mesh_shape):
    wide, narrow = mesh_shape["wide"], mesh_shape["narrow"]
    return (wide // 2, 2, narrow // 2, 2)


class Gather:
    def __init__(self, dims, families):
        self.dims = dims
        wide, narrow = lax.axis_index("wide"), lax.axis_index("narrow")
        self.at = (wide // dims[1], lax.rem(wide, dims[1]), narrow // dims[3], lax.rem(narrow, dims[3]))
        self.families = families

    def device(self, dim, index):
        at = list(self.at)
        at[dim] = index
        return (at[0] * self.dims[1] + at[1], at[2] * self.dims[3] + at[3])

    def greet(self):
        barrier = pltpu.get_barrier_semaphore()
        count = 0
        for dim, size in enumerate(self.dims):
            for step in range(1, size):
                peer = self.device(dim, lax.rem(self.at[dim] + step, size))
                pl.semaphore_signal(barrier, inc=1, device_id=peer, device_id_type=MESH)
                count += 1
        pl.semaphore_wait(barrier, count)

    def view(self, family, j, stage, index):
        _, target, order, _, _, _ = family
        done, dim = order[:stage], order[stage]
        return target.at[
            (j,) + tuple(slice(None) if d in done else (index if d == dim else self.at[d]) for d in range(4))
        ]

    def own(self, family, j):
        source, target, _, _, _, own = family
        return pltpu.make_async_copy(source.at[j], target.at[(j,) + self.at], own.at[j])

    def start(self, j, stage):
        for family in self.families:
            source, _, order, send, recv, _ = family
            dim = order[stage]
            size = self.dims[dim]
            if stage == 0:
                self.own(family, j).start()
            mine = self.view(family, j, stage, self.at[dim])
            for step in range(1, size):
                pltpu.make_async_remote_copy(
                    src_ref=source.at[j] if stage == 0 else mine,
                    dst_ref=mine,
                    send_sem=send.at[j, stage],
                    recv_sem=recv.at[j, stage],
                    device_id=self.device(dim, lax.rem(self.at[dim] + step, size)),
                    device_id_type=MESH,
                ).start()

    def whole(self, family, j, stage):
        _, _, order, send, recv, _ = family
        size = self.dims[order[stage]]
        part = self.view(family, j, stage, pl.ds(0, size - 1))
        return pltpu.make_async_remote_copy(
            src_ref=part, dst_ref=part, send_sem=send.at[j, stage], recv_sem=recv.at[j, stage],
            device_id=self.device(order[stage], lax.rem(self.at[order[stage]] + 1, size)), device_id_type=MESH,
        )

    def arrive(self, j, stage):
        for family in self.families:
            if stage == 0:
                self.own(family, j).wait()
            self.whole(family, j, stage).wait_recv()

    def finish(self, count):
        @pl.loop(0, count)
        def _(j):
            for family in self.families:
                for stage in range(4):
                    self.whole(family, j, stage).wait_send()

    def tick(self, t, count):
        @pl.when(t + AHEAD < count)
        def _():
            self.start(t + AHEAD, 0)

        for stage in (2, 1, 0):
            j = t - LAG * stage

            @pl.when((j >= 0) & (j < count))
            def _():
                self.arrive(j, stage)
                self.start(j, stage + 1)

        j = t - LAG * 3

        @pl.when((j >= 0) & (j < count))
        def _():
            self.arrive(j, 3)


XY, YX = (0, 1, 2, 3), (0, 2, 1, 3)


def norm_parts(values):
    center = values - jnp.mean(values, axis=-1, keepdims=True)
    rate = lax.rsqrt(jnp.mean(center * center, axis=-1, keepdims=True) + 1e-05)
    return center * rate, rate


def norm_back(hat, rate, grad, gain):
    inner = grad * gain
    return rate * (
        inner - jnp.mean(inner, axis=-1, keepdims=True) - hat * jnp.mean(inner * hat, axis=-1, keepdims=True)
    )


ROOT = math.sqrt(2.0 / math.pi)


def gelu_both(v):
    square = v * v
    th = jnp.tanh(ROOT * v * (1.0 + 0.044715 * square))
    half = 0.5 * (1.0 + th)
    slope = half + 0.5 * v * (1.0 - th * th) * (ROOT * (1.0 + 3 * 0.044715 * square))
    return v * half, slope


def ff_kernel(dims, x_hbm, cot_hbm, att_hbm, wo_hbm, e_hbm, c_hbm, bo_ref, be_ref, bc_ref, gain_ref, shift_ref,
              out_hbm, gm_hbm, ga_hbm,
              ew, cw, x, cot, att, wo, n2, mid, acc, gacc,
              e_send, e_recv, e_own, c_send, c_recv, c_own, in_sems, out_sems):
    length, width = x.shape
    count = e_hbm.shape[0]
    gather = Gather(dims, [(e_hbm, ew, XY, e_send, e_recv, e_own), (c_hbm, cw, YX, c_send, c_recv, c_own)])
    loads = [
        pltpu.make_async_copy(src, dst, in_sems.at[n])
        for n, (src, dst) in enumerate(((x_hbm, x), (att_hbm, att), (wo_hbm, wo), (cot_hbm, cot)))
    ]
    for load in loads:
        load.start()
    gather.greet()
    for j in range(min(AHEAD, count)):
        gather.start(j, 0)
    for load in loads:
        load.wait()
    gain, shift = gain_ref[...], shift_ref[...]
    tiles = length // TILE

    def rows_of(i):
        return pl.ds(pl.multiple_of(i * TILE, TILE), TILE)

    def before(i):
        rows = rows_of(i)
        value = x[rows, :].astype(F32) + (dot_nn(att[rows, :], wo[...]) + bo_ref[...])
        mid[rows, :] = value
        hat, _ = norm_parts(value)
        n2[rows, :] = (hat * gain + shift).astype(BF16)
        acc[rows, :] = jnp.zeros((TILE, width), F32)
        gacc[rows, :] = jnp.zeros((TILE, width), F32)

    def chunk(j):
        e = ew.at[j]
        c = cw.at[j]
        bias = be_ref[pl.ds(j, 1), :]

        @pl.loop(0, tiles)
        def _(i):
            rows = rows_of(i)
            ev = e[...].reshape(width, -1)
            cv = c[...].reshape(-1, width)
            active, slope = gelu_both(dot_nn(n2[rows, :], ev) + bias)
            grad = (dot_nt(cot[rows, :], cv) * slope).astype(BF16)
            acc[rows, :] += dot_nn(active.astype(BF16), cv)
            gacc[rows, :] += dot_nt(grad, ev)

    @pl.loop(0, max(count + 3 * LAG, tiles))
    def _(t):
        gather.tick(t, count)

        @pl.when(t < tiles)
        def _():
            before(t)

        j = t - 3 * LAG

        @pl.when((j >= 0) & (j < count))
        def _():
            chunk(j)

    def stores(i):
        rows = rows_of(i)
        return [
            pltpu.make_async_copy(src.at[rows, :], dst.at[rows, :], out_sems.at[n, i])
            for n, (src, dst) in enumerate(((x, out_hbm), (gacc, gm_hbm), (att, ga_hbm)))
        ]

    @pl.loop(0, tiles)
    def _(i):
        rows = rows_of(i)
        value = mid[rows, :]
        x[rows, :] = (value + (acc[rows, :] + bc_ref[...])).astype(BF16)
        hat, rate = norm_parts(value)
        grad = cot[rows, :].astype(F32) + norm_back(hat, rate, gacc[rows, :], gain)
        gacc[rows, :] = grad
        att[rows, :] = dot_nt(grad.astype(BF16), wo[...]).astype(BF16)
        for store in stores(i):
            store.start()

    gather.finish(count)

    @pl.loop(0, tiles)
    def _(i):
        for store in stores(i):
            store.wait()


def feed_forward(dims, x, cot, attended, full_output, e_shard, c_shard, bo, be, bc, gain, shift):
    length, width = x.shape
    chunks = e_shard.shape[0]
    columns = be.shape[1]
    anyspace = pl.BlockSpec(memory_space=pl.ANY)
    vmem = pl.BlockSpec(memory_space=pltpu.VMEM)
    dma = pltpu.SemaphoreType.DMA
    full = lambda kind: pltpu.VMEM((length, width), kind)
    return pl.pallas_call(
        functools.partial(ff_kernel, dims),
        in_specs=[anyspace] * 6 + [vmem] * 5,
        out_specs=[anyspace] * 3,
        out_shape=[jax.ShapeDtypeStruct((length, width), kind) for kind in (BF16, F32, BF16)],
        scratch_shapes=[
            pltpu.VMEM((chunks,) + dims + e_shard.shape[1:], BF16),
            pltpu.VMEM((chunks,) + dims + c_shard.shape[1:], BF16),
            full(BF16), full(BF16), full(BF16), pltpu.VMEM((width, width), BF16),
            full(BF16), full(F32), full(F32), full(F32),
            dma((chunks, 4)), dma((chunks, 4)), dma((chunks,)),
            dma((chunks, 4)), dma((chunks, 4)), dma((chunks,)),
            dma((4,)), dma((3, length // TILE)),
        ],
        compiler_params=pltpu.CompilerParams(collective_id=1, has_side_effects=True, vmem_limit_bytes=58 << 20),
        name="feed_forward",
    )(x, cot, attended, full_output, e_shard, c_shard, bo, be, bc, gain, shift)


def back_kernel(dims, prefix, most, count, len_ref, q_ref, k_ref, v_ref, pk_ref, pv_ref, do_ref, o_ref, lse_ref,
                gain_ref, w_hbm, x_hbm, gm_hbm, gx_hbm, total_ref,
                dk_acc, dv_acc, dpk, dpv, gmix, w, x, gm, tiles, inbox, sums,
                in_sems, out_sems, give_send, give_recv, tell_send, tell_recv):
    length = q_ref.shape[0]
    width = x.shape[1]
    pair = pl.program_id(0)
    pairs = width // 128
    devices = math.prod(dims)
    narrow_size = dims[2] * dims[3]
    me = lax.axis_index("wide") * narrow_size + lax.axis_index("narrow")
    tile_count = 4 * pairs
    ratio = devices // tile_count
    owns = lax.rem(me, ratio) == 0
    own_tile = me // ratio
    place = lambda device: (device // narrow_size, lax.rem(device, narrow_size))
    loads = [
        pltpu.make_async_copy(src, dst, in_sems.at[n])
        for n, (src, dst) in enumerate(((w_hbm, w), (x_hbm, x), (gm_hbm, gm)))
    ]
    barrier = pltpu.get_barrier_semaphore()

    @pl.when(pair == 0)
    def _():
        for load in loads:
            load.start()

        @pl.loop(1, devices)
        def _(step):
            peer = place(lax.rem(me + step, devices))
            pl.semaphore_signal(barrier, inc=1, device_id=peer, device_id_type=MESH)

    start = start_row(len_ref, count, length)
    lane = lax.broadcasted_iota(jnp.int32, (1, 128), 1)
    pre_seen = lax.broadcasted_iota(jnp.int32, (PAD, BLOCK), 0) < prefix
    pk, pv = pk_ref[...], pv_ref[...]
    k_t = k_ref[...].T
    pk_t = pk.T
    head_of = lax.broadcasted_iota(jnp.int32, (8, 128), 0)
    pick = ((lax.broadcasted_iota(jnp.int32, (8, 128), 1) // 64) == head_of).astype(F32).astype(BF16)
    columns = [pl.ds(pl.multiple_of(part * width + pair * 128, 128), 128) for part in range(3)]
    for qi in range(length // BLOCK):
        rows = slice(qi * BLOCK, (qi + 1) * BLOCK)
        lo = span(qi, most)
        st = start[:, rows]
        q2 = q_ref[rows, :] * jnp.asarray(0.125, BF16)
        do2 = do_ref[rows, :]
        prod = do2.astype(F32) * o_ref[rows, :].astype(F32)
        high = prod.astype(BF16)
        low = (prod - high.astype(F32)).astype(BF16)
        delta2 = dot_nt(pick, high) + dot_nt(pick, low)
        halves = []
        for h in range(2):
            mine = (lane // 64) == h
            qh = jnp.where(mine, q2, jnp.zeros((), BF16))
            doh = jnp.where(mine, do2, jnp.zeros((), BF16))
            lse = lse_ref[0, h:h + 1, rows]
            delta = delta2[h:h + 1]
            p = jnp.where(pre_seen, jnp.exp(dot_nt(pk, qh) - lse), 0.0)
            ds = (p * (dot_nt(pv, doh) - delta)).astype(BF16)
            one_dpk = dot_nn(ds, qh)
            one_dpv = dot_nn(p.astype(BF16), doh)
            if qi == 0 and h == 0:
                dpk[...], dpv[...] = one_dpk, one_dpv
            else:
                dpk[...] += one_dpk
                dpv[...] += one_dpv
            dq = dot_nn(pk_t[h * 64:(h + 1) * 64], ds)
            for kj in range(lo, qi + 1):
                keys = slice(kj * BLOCK, (kj + 1) * BLOCK)
                s = dot_nt(k_ref[keys, :], qh)
                p = jnp.exp(s - lse)
                p = jnp.where(visible(st, kj * BLOCK, BLOCK, qi * BLOCK, BLOCK, kj == qi), p, 0.0)
                dp = dot_nt(v_ref[keys, :], doh)
                ds = (p * (dp - delta)).astype(BF16)
                dv = dot_nn(p.astype(BF16), doh)
                dk = dot_nn(ds, qh)
                if kj == qi and h == 0:
                    dv_acc[keys, :], dk_acc[keys, :] = dv, dk
                else:
                    dv_acc[keys, :] += dv
                    dk_acc[keys, :] += dk
                dq = dq + dot_nn(k_t[h * 64:(h + 1) * 64, keys], ds)
            halves.append(dq * 0.125)
        gmix[rows, columns[0]] = jnp.concatenate(halves, axis=0).T.astype(BF16)
    gmix[:, columns[1]] = dk_acc[...].astype(BF16)
    gmix[:, columns[2]] = dv_acc[...].astype(BF16)

    def give(part):
        tile = part * pairs + pair
        return pltpu.make_async_remote_copy(
            src_ref=tiles.at[tile], dst_ref=inbox.at[me], send_sem=give_send, recv_sem=give_recv,
            device_id=place(tile * ratio), device_id_type=MESH,
        )

    @pl.when(pair == 0)
    def _():
        pl.semaphore_wait(barrier, devices - 1)

    for part, (ref, half) in enumerate(((dpk, 0), (dpk, 1), (dpv, 0), (dpv, 1))):
        value = ref[half * 8:(half + 1) * 8, :]
        tile = part * pairs + pair
        tiles[pl.ds(tile, 1)] = value[None]
        to_me = owns & (tile == own_tile)

        @pl.when(to_me)
        def _():
            inbox[pl.ds(me, 1)] = value[None]

        @pl.when(jnp.logical_not(to_me))
        def _():
            give(part).start()

    @pl.when(pair == pairs - 1)
    def _():
        for load in loads:
            load.wait()
        tall = 256

        def store(i):
            rows = pl.ds(i * tall, tall)
            return pltpu.make_async_copy(x.at[rows, :], gx_hbm.at[rows, :], out_sems.at[i])

        def finish_rows(i):
            rows = pl.ds(i * tall, tall)
            grad = dot_nt(gmix[rows, :], w[...])
            hat, rate = norm_parts(x[rows, :].astype(F32))
            x[rows, :] = (gm[rows, :] + norm_back(hat, rate, grad, gain_ref[...])).astype(BF16)
            store(i).start()

        def bytes_of(ref, n, send, recv):
            part = ref.at[pl.ds(0, n)]
            return pltpu.make_async_remote_copy(
                src_ref=part, dst_ref=part, send_sem=send, recv_sem=recv,
                device_id=place(lax.rem(me + 1, devices)), device_id_type=MESH,
            )

        finish_rows(0)
        finish_rows(1)

        @pl.when(owns)
        def _():
            bytes_of(inbox, devices - 1, give_send, give_recv).wait_recv()
            summed = inbox[0]
            for device in range(1, devices):
                summed = summed + inbox[device]
            sums[pl.ds(own_tile, 1)] = summed[None]

            @pl.loop(1, devices)
            def _(step):
                pltpu.make_async_remote_copy(
                    src_ref=sums.at[own_tile], dst_ref=sums.at[own_tile], send_sem=tell_send,
                    recv_sem=tell_recv, device_id=place(lax.rem(me + step, devices)), device_id_type=MESH,
                ).start()

        finish_rows(2)
        finish_rows(3)

        @pl.when(owns)
        def _():
            bytes_of(tiles, tile_count - 1, give_send, give_recv).wait_send()
            bytes_of(inbox, devices - 1, tell_send, tell_recv).wait_send()
            bytes_of(tiles, tile_count - 1, tell_send, tell_recv).wait_recv()

        @pl.when(jnp.logical_not(owns))
        def _():
            bytes_of(tiles, tile_count, give_send, give_recv).wait_send()
            bytes_of(tiles, tile_count, tell_send, tell_recv).wait_recv()

        total_ref[...] = sums[...]
        for i in range(length // tall):
            store(i).wait()


def attend_back(dims, mixed, lengths, pre, grad, attended, lse, gain, full_mixer, x, grad_middle, prefix, most):
    length, width = grad.shape
    pairs = width // 128
    count = lengths.shape[1]
    devices = math.prod(dims)
    col = lambda off: pl.BlockSpec((length, 128), lambda p: (0, p + off))
    pcol = lambda off: pl.BlockSpec((PAD, 128), lambda p: (0, p + off))
    anyspace = pl.BlockSpec(memory_space=pl.ANY)
    dma = pltpu.SemaphoreType.DMA
    return pl.pallas_call(
        functools.partial(back_kernel, dims, prefix, most, count),
        grid=(pairs,),
        in_specs=[pl.BlockSpec(memory_space=pltpu.SMEM), col(0), col(pairs), col(2 * pairs), pcol(0), pcol(pairs),
                  col(0), col(0), pl.BlockSpec((1, 2, length), lambda p: (p, 0, 0)),
                  pl.BlockSpec((1, width), lambda p: (0, 0)), anyspace, anyspace, anyspace],
        out_specs=[anyspace, pl.BlockSpec((4 * pairs, 8, 128), lambda p: (0, 0, 0))],
        out_shape=[jax.ShapeDtypeStruct((length, width), BF16), jax.ShapeDtypeStruct((4 * pairs, 8, 128), F32)],
        scratch_shapes=[pltpu.VMEM((length, 128), F32)] * 2 + [pltpu.VMEM((PAD, 128), F32)] * 2 + [
            pltpu.VMEM((length, 3 * width), BF16), pltpu.VMEM((width, 3 * width), BF16),
            pltpu.VMEM((length, width), BF16), pltpu.VMEM((length, width), F32),
            pltpu.VMEM((4 * pairs, 8, 128), F32), pltpu.VMEM((devices, 8, 128), F32),
            pltpu.VMEM((4 * pairs, 8, 128), F32),
            dma((3,)), dma((length // 256,)), dma(()), dma(()), dma(()), dma(()),
        ],
        compiler_params=pltpu.CompilerParams(collective_id=2, has_side_effects=True, vmem_limit_bytes=56 << 20),
        name="attend_back",
    )(lengths, mixed, mixed, mixed, pre, pre, grad, attended, lse, gain, full_mixer, x, grad_middle)


def split(value):
    high = value.astype(BF16)
    return high, (value - high.astype(F32)).astype(BF16)


def dot_fine(left, right, dims):
    lh, ll = split(left)
    rh, rl = split(right)
    one = lambda a, b: lax.dot_general(a, b, (dims, ((), ())), preferred_element_type=F32)
    return one(lh, rh) + (one(lh, rl) + one(ll, rh))


def reparam_kernel(prefix, total_ref, sq_ref, embed_ref, ro_ref, ri_ref, gx_hbm, out_hbm,
                   gx_out, out_out, ge_ref, gi_ref, gib_ref, go_ref, gob_ref, gs, sems):
    step = pl.program_id(0)
    steps = pl.num_programs(0)
    pairs = total_ref.shape[0] // 4
    moves = [pltpu.make_async_copy(gx_hbm, gx_out, sems.at[0]), pltpu.make_async_copy(out_hbm, out_out, sems.at[1])]

    @pl.when(step == 0)
    def _():
        for move in moves:
            move.start()
        gs[...] = jnp.zeros_like(gs)

    per = 2 * pairs // steps
    blocks = []
    for n in range(per):
        block = step * per + n
        part, pair = block // pairs, lax.rem(block, pairs)
        top = total_ref[pl.ds(2 * part * pairs + pair, 1)][0]
        low = total_ref[pl.ds((2 * part + 1) * pairs + pair, 1)][0]
        blocks.append(jnp.concatenate([top, low], axis=0))
    grad = jnp.concatenate(blocks, axis=1)
    go_ref[...] = dot_fine(sq_ref[...], grad, ((0,), (0,)))
    gob_ref[...] = jnp.sum(grad, axis=0, keepdims=True)
    gs[...] += dot_fine(grad, ro_ref[...], ((1,), (1,)))

    @pl.when(step == steps - 1)
    def _():
        squashed = sq_ref[...]
        inner = gs[...] * (1.0 - squashed * squashed)
        gi_ref[...] = dot_fine(embed_ref[...], inner, ((0,), (0,)))
        gib_ref[...] = jnp.sum(inner, axis=0, keepdims=True)
        ge_ref[...] = dot_fine(inner, ri_ref[...], ((1,), (1,)))[:prefix]
        for move in moves:
            move.wait()


def reparam_back(total, squashed, embed, reparam_out, reparam_in, grad_tokens, out_tokens, prefix):
    width2 = reparam_out.shape[1]
    rep = reparam_out.shape[0]
    width = embed.shape[1]
    steps = 4
    whole = lambda array: pl.BlockSpec(array.shape, lambda i: (0,) * array.ndim)
    anyspace = pl.BlockSpec(memory_space=pl.ANY)
    shape = jax.ShapeDtypeStruct
    return pl.pallas_call(
        functools.partial(reparam_kernel, prefix),
        grid=(steps,),
        in_specs=[whole(total), whole(squashed), whole(embed), pl.BlockSpec((rep, width2 // steps), lambda i: (0, i)),
                  whole(reparam_in), anyspace, anyspace],
        out_specs=[anyspace, anyspace,
                   pl.BlockSpec((prefix, width), lambda i: (0, 0)), pl.BlockSpec((width, rep), lambda i: (0, 0)),
                   pl.BlockSpec((1, rep), lambda i: (0, 0)), pl.BlockSpec((rep, width2 // steps), lambda i: (0, i)),
                   pl.BlockSpec((1, width2 // steps), lambda i: (0, i))],
        out_shape=[shape(grad_tokens.shape, BF16), shape(out_tokens.shape, BF16), shape((prefix, width), F32),
                   shape((width, rep), F32), shape((1, rep), F32), shape((rep, width2), F32), shape((1, width2), F32)],
        scratch_shapes=[pltpu.VMEM(squashed.shape, F32), pltpu.SemaphoreType.DMA((2,))],
        compiler_params=pltpu.CompilerParams(vmem_limit_bytes=40 << 20),
        name="reparam_back",
    )(total, squashed, embed, reparam_out, reparam_in, grad_tokens, out_tokens)


def shards(
    dims,
    tokens,
    lengths,
    cotangent,
    mixer_weight,
    output_weight,
    expand_weight,
    contract_weight,
    mixer_bias,
    output_bias,
    expand_bias,
    contract_bias,
    norm_gains,
    norm_shifts,
    prefix_embed,
    reparam_in,
    reparam_in_bias,
    reparam_out,
    reparam_out_bias,
):
    row_count, length, model_width = tokens.shape
    total_rows = row_count * length
    full_mixer = lax.all_gather(mixer_weight, ("wide", "narrow"), axis=0, tiled=True)
    full_output = lax.all_gather(output_weight, ("wide", "narrow"), axis=0, tiled=True)
    devices = math.prod(dims)
    hidden = expand_weight.shape[1]
    part = hidden // devices // CHUNKS
    by_chunk = lambda array: array.reshape(-1, devices, CHUNKS, part).transpose(2, 0, 1, 3).reshape(CHUNKS, -1, devices * part)
    expand_parts = by_chunk(expand_weight)
    expand_bias_parts = by_chunk(expand_bias)[:, 0]
    contract_parts = contract_weight.reshape(CHUNKS, part, model_width)
    prefix_count = prefix_embed.shape[0]
    tall = lambda array: jnp.pad(array, ((0, PAD - prefix_count), (0, 0)))
    squashed = jnp.tanh(
        jnp.dot(prefix_embed, reparam_in, precision=lax.Precision.HIGHEST) + reparam_in_bias
    )
    prefix_kv = jnp.dot(squashed, reparam_out, precision=lax.Precision.HIGHEST) + reparam_out_bias
    pre = tall(prefix_kv.astype(jnp.bfloat16))
    inputs = tokens.reshape(total_rows, model_width).astype(jnp.float32)
    normed_one = norm_layer(inputs, norm_gains[0], norm_shifts[0])
    mixed = (
        jnp.dot(normed_one.astype(jnp.bfloat16), full_mixer, preferred_element_type=jnp.float32)
        + mixer_bias
    )
    mixed_low = mixed.astype(jnp.bfloat16)
    attended, log_sums = attend(mixed_low, lengths, pre, prefix_count, MOST)
    as_row = lambda array: array.reshape(1, -1)
    out_tokens, grad_middle, grad_attended = feed_forward(
        dims, tokens.reshape(total_rows, model_width), cotangent.reshape(total_rows, model_width), attended, full_output,
        expand_parts, contract_parts, as_row(output_bias), expand_bias_parts, as_row(contract_bias),
        norm_gains[1:2], norm_shifts[1:2],
    )
    grad_tokens, total = attend_back(
        dims, mixed_low, lengths, pre, grad_attended, attended, log_sums, norm_gains[0:1], full_mixer,
        tokens.reshape(total_rows, model_width), grad_middle, prefix_count, MOST,
    )
    grad_tokens, out_tokens, grad_embed, grad_in, grad_in_bias, grad_out, grad_out_bias = reparam_back(
        total, tall(squashed), tall(prefix_embed), reparam_out, reparam_in, grad_tokens, out_tokens, prefix_count
    )
    return (
        out_tokens.reshape(tokens.shape), grad_tokens.reshape(tokens.shape), grad_embed, grad_in, grad_in_bias[0],
        grad_out, grad_out_bias[0],
    )


def solution(mesh):
    return jax.shard_map(
        functools.partial(shards, grid_dims(mesh.shape)),
        mesh=mesh,
        in_specs=(
            P(("wide", "narrow"), None, None),
            P(("wide", "narrow"), None),
            P(("wide", "narrow"), None, None),
            P(("wide", "narrow"), None),
            P(("wide", "narrow"), None),
            P(("wide", "narrow"), None),
            P(("wide", "narrow"), None),
            P(),
            P(),
            P(),
            P(),
            P(),
            P(),
            P(),
            P(),
            P(),
            P(),
            P(),
        ),
        out_specs=(
            P(("wide", "narrow"), None, None),
            P(("wide", "narrow"), None, None),
            P(),
            P(),
            P(),
            P(),
            P(),
        ),
        check_vma=False,
    )
```

```python
import functools
import math

import jax
import jax.numpy as jnp
from jax import lax
from jax.experimental import pallas as pl
from jax.experimental.pallas import tpu as pltpu
from jax.sharding import PartitionSpec as P

MOST = 512


BLOCK = 256
PAD = 16
F32, BF16 = jnp.float32, jnp.bfloat16


def dot_nt(a, b):
    return lax.dot_general(a, b, (((1,), (1,)), ((), ())), preferred_element_type=F32)


def dot_nn(a, b):
    return lax.dot_general(a, b, (((1,), (0,)), ((), ())), preferred_element_type=F32)


def start_row(lengths_ref, count, length):
    place = lax.broadcasted_iota(jnp.int32, (1, length), 1)
    start = jnp.zeros((1, length), jnp.int32)
    total = jnp.int32(0)
    for j in range(count):
        total = total + lengths_ref[0, j]
        start = jnp.where(place >= total, total, start)
    return start


def visible(start, first_key, keys, first_query, queries, diagonal):
    key = lax.broadcasted_iota(jnp.int32, (keys, queries), 0) + first_key
    seen = key >= start
    if diagonal:
        query = lax.broadcasted_iota(jnp.int32, (keys, queries), 1) + first_query
        seen = seen & (key <= query)
    return seen


def span(qi, most):
    return max(0, qi - most // BLOCK)


def fwd_pair(q2, k_ref, v_ref, pk, pv, start, prefix, most, o_ref, lse_ref):
    length = q2.shape[0]
    lane = lax.broadcasted_iota(jnp.int32, (1, 128), 1)
    pre_seen = lax.broadcasted_iota(jnp.int32, (PAD, BLOCK), 0) < prefix
    v_t = v_ref[...].T
    pv_t = pv.T
    for qi in range(length // BLOCK):
        rows = slice(qi * BLOCK, (qi + 1) * BLOCK)
        lo = span(qi, most)
        st = start[:, rows]
        halves = []
        for h in range(2):
            qh = jnp.where((lane // 64) == h, q2[rows], jnp.zeros((), BF16))
            s_pre = jnp.where(pre_seen, dot_nt(pk, qh), -1e30)
            peak = jnp.max(s_pre, axis=0, keepdims=True)
            parts = []
            for kj in range(lo, qi + 1):
                s = dot_nt(k_ref[kj * BLOCK:(kj + 1) * BLOCK, :], qh)
                s = jnp.where(visible(st, kj * BLOCK, BLOCK, qi * BLOCK, BLOCK, kj == qi), s, -1e30)
                peak = jnp.maximum(peak, jnp.max(s, axis=0, keepdims=True))
                parts.append(s)
            p = jnp.exp(s_pre - peak)
            total = jnp.sum(p, axis=0, keepdims=True)
            o = dot_nn(pv_t[h * 64:(h + 1) * 64], p.astype(BF16))
            for n, kj in enumerate(range(lo, qi + 1)):
                p = jnp.exp(parts[n] - peak)
                total = total + jnp.sum(p, axis=0, keepdims=True)
                o = o + dot_nn(v_t[h * 64:(h + 1) * 64, kj * BLOCK:(kj + 1) * BLOCK], p.astype(BF16))
            halves.append(o / total)
            lse_ref[h:h + 1, rows] = peak + jnp.log(total)
        o_ref[rows, :] = jnp.concatenate(halves, axis=0).T.astype(BF16)


CHUNKS = 8
TILE = 256
MESH = pl.DeviceIdType.MESH
XY, YX = (0, 1, 2, 3), (0, 2, 1, 3)


def grid_dims(mesh_shape):
    wide, narrow = mesh_shape["wide"], mesh_shape["narrow"]
    return (wide // 2, 2, narrow // 2, 2)


class Family:
    def __init__(self, source, target, order, sems, count, first=0, stride=1, offset=0, pace=1, lag=1, ahead=3):
        self.source, self.target, self.order = source, target, order
        self.send, self.recv, self.own = sems
        self.count, self.first, self.stride = count, first, stride
        self.offset, self.pace, self.lag, self.ahead = offset, pace, lag, ahead

    def block(self, j):
        return self.first + self.stride * j

    def end(self):
        return self.offset + self.pace * (self.count - 1) + 3 * self.lag + 1


class Gather:
    def __init__(self, dims, families):
        self.dims = dims
        wide, narrow = lax.axis_index("wide"), lax.axis_index("narrow")
        self.at = (wide // dims[1], lax.rem(wide, dims[1]), narrow // dims[3], lax.rem(narrow, dims[3]))
        self.families = families

    def device(self, dim, index):
        at = list(self.at)
        at[dim] = index
        return (at[0] * self.dims[1] + at[1], at[2] * self.dims[3] + at[3])

    def greet(self):
        barrier = pltpu.get_barrier_semaphore()
        count = 0
        for dim, size in enumerate(self.dims):
            for step in range(1, size):
                peer = self.device(dim, lax.rem(self.at[dim] + step, size))
                pl.semaphore_signal(barrier, inc=1, device_id=peer, device_id_type=MESH)
                count += 1
        pl.semaphore_wait(barrier, count)

    def view(self, family, j, stage, index):
        done, dim = family.order[:stage], family.order[stage]
        return family.target.at[
            (family.block(j),)
            + tuple(slice(None) if d in done else (index if d == dim else self.at[d]) for d in range(4))
        ]

    def keep(self, family, j):
        block = family.block(j)
        return pltpu.make_async_copy(family.source.at[block], family.target.at[(block,) + self.at], family.own.at[j])

    def start(self, family, j, stage):
        dim = family.order[stage]
        size = self.dims[dim]
        if stage == 0:
            self.keep(family, j).start()
        mine = self.view(family, j, stage, self.at[dim])
        for step in range(1, size):
            pltpu.make_async_remote_copy(
                src_ref=family.source.at[family.block(j)] if stage == 0 else mine,
                dst_ref=mine,
                send_sem=family.send.at[j, stage],
                recv_sem=family.recv.at[j, stage],
                device_id=self.device(dim, lax.rem(self.at[dim] + step, size)),
                device_id_type=MESH,
            ).start()

    def whole(self, family, j, stage):
        dim = family.order[stage]
        size = self.dims[dim]
        part = self.view(family, j, stage, pl.ds(0, size - 1))
        return pltpu.make_async_remote_copy(
            src_ref=part, dst_ref=part, send_sem=family.send.at[j, stage], recv_sem=family.recv.at[j, stage],
            device_id=self.device(dim, lax.rem(self.at[dim] + 1, size)), device_id_type=MESH,
        )

    def arrive(self, family, j, stage):
        if stage == 0:
            self.keep(family, j).wait()
        self.whole(family, j, stage).wait_recv()

    def begin(self):
        for family in self.families:
            for j in range(family.count):
                if family.offset + family.pace * j < family.ahead:
                    self.start(family, j, 0)

    def tick(self, t):
        for stage in (3, 2, 1, 0, -1):
            for family in self.families:
                past = t - family.offset - (family.lag * stage if stage >= 0 else -family.ahead)
                j = past // family.pace

                @pl.when((past >= 0) & (j < family.count) & (lax.rem(past, family.pace) == 0))
                def _():
                    if stage >= 0:
                        self.arrive(family, j, stage)
                    if stage < 3:
                        self.start(family, j, stage + 1)

    def finish(self):
        for family in self.families:

            @pl.loop(0, family.count)
            def _(j):
                for stage in range(4):
                    self.whole(family, j, stage).wait_send()


def gather_sems(count):
    dma = pltpu.SemaphoreType.DMA
    return [dma((count, 4)), dma((count, 4)), dma((count,))]


def norm_parts(values):
    center = values - jnp.mean(values, axis=-1, keepdims=True)
    rate = lax.rsqrt(jnp.mean(center * center, axis=-1, keepdims=True) + 1e-05)
    return center * rate, rate


def norm_back(hat, rate, grad, gain):
    inner = grad * gain
    return rate * (
        inner - jnp.mean(inner, axis=-1, keepdims=True) - hat * jnp.mean(inner * hat, axis=-1, keepdims=True)
    )


def split(value):
    high = value.astype(BF16)
    return high, (value - high.astype(F32)).astype(BF16)


def dot_fine(left, right, dims):
    lh, ll = split(left)
    rh, rl = split(right)
    one = lambda a, b: lax.dot_general(a, b, (dims, ((), ())), preferred_element_type=F32)
    return one(lh, rh) + (one(lh, rl) + one(ll, rh))


ROOT = math.sqrt(2.0 / math.pi)


def gelu_both(v):
    square = v * v
    th = jnp.tanh(ROOT * v * (1.0 + 0.044715 * square))
    half = 0.5 * (1.0 + th)
    slope = half + 0.5 * v * (1.0 - th * th) * (ROOT * (1.0 + 3 * 0.044715 * square))
    return v * half, slope


PAIR_TICK = 3
FF_TICK = 12


def layer_kernel(dims, prefix, most, count, len_ref, x_hbm, cot_hbm, m_hbm, w_hbm, e_hbm, c_hbm, ri_hbm, ro_hbm,
                 embed_ref, rib_ref, rob_ref, mb_ref, bo_ref, be_ref, bc_ref, gain_ref, shift_ref,
                 mixed_hbm, att_hbm, lse_ref, pre_ref, sq_ref, mixer_hbm, out_hbm, gm_hbm, ga_hbm,
                 x, norm, mixer, mixed, att, cot, wo, mid, acc, gacc, ew, cw,
                 m0_send, m0_recv, m0_own, m1_send, m1_recv, m1_own, w0_send, w0_recv, w0_own, w1_send, w1_recv, w1_own,
                 e_send, e_recv, e_own, c_send, c_recv, c_own,
                 in_sems, mixed_sems, att_sems, mixer_sems, out_sems):
    length, width = x.shape
    pairs, chunks = m_hbm.shape[0], e_hbm.shape[0]
    rep = sq_ref.shape[1]
    half = pairs // 2
    gather = Gather(dims, [
        Family(m_hbm, mixer, XY, (m0_send, m0_recv, m0_own), half, first=0, stride=2, offset=0, pace=2),
        Family(m_hbm, mixer, YX, (m1_send, m1_recv, m1_own), half, first=1, stride=2, offset=1, pace=2),
        Family(w_hbm, wo, XY, (w0_send, w0_recv, w0_own), 1, first=0, offset=FF_TICK - 6),
        Family(w_hbm, wo, YX, (w1_send, w1_recv, w1_own), 1, first=1, offset=FF_TICK - 6),
        Family(e_hbm, ew, XY, (e_send, e_recv, e_own), chunks, offset=FF_TICK - 6, lag=2),
        Family(c_hbm, cw, YX, (c_send, c_recv, c_own), chunks, offset=FF_TICK - 6, lag=2),
    ])
    loads = [
        pltpu.make_async_copy(src, dst, in_sems.at[n])
        for n, (src, dst) in enumerate((
            (x_hbm, x), (ri_hbm, mid.at[:, :rep]), (ro_hbm.at[:, :width], acc.at[:rep]), (ro_hbm.at[:, width:], gacc.at[:rep]),
            (cot_hbm, cot),
        ))
    ]
    for load in loads:
        load.start()
    gather.greet()
    gather.begin()
    tiles = length // TILE

    def rows_of(i):
        return pl.ds(pl.multiple_of(i * TILE, TILE), TILE)

    def first_norm():
        loads[0].wait()

        @pl.loop(0, tiles)
        def _(i):
            rows = rows_of(i)
            hat, _ = norm_parts(x[rows, :].astype(F32))
            norm[rows, :] = (hat * gain_ref[0:1, :] + shift_ref[0:1, :]).astype(BF16)

    def prefix_rows():
        for load in loads[1:]:
            load.wait()
        seen = lax.broadcasted_iota(jnp.int32, (PAD, 1), 0) < prefix
        squashed = jnp.where(seen, jnp.tanh(dot_fine(embed_ref[...], mid[:, :rep], ((1,), (0,))) + rib_ref[...]), 0.0)
        sq_ref[...] = squashed
        for part, ref in enumerate((acc, gacc)):
            columns = slice(part * width, (part + 1) * width)
            whole = dot_fine(squashed, ref[:rep, :], ((1,), (0,))) + rob_ref[:, columns]
            pre_ref[:, columns] = jnp.where(seen, whole, 0.0).astype(BF16)

    def stores(p, slot):
        columns = pl.ds(pl.multiple_of(p * 128, 128), 128)
        return [
            pltpu.make_async_copy(mixed.at[slot], mixed_hbm.at[p], mixed_sems.at[slot]),
            pltpu.make_async_copy(att.at[:, columns], att_hbm.at[:, columns], att_sems.at[slot]),
        ]

    def keep_mixer(p):
        return pltpu.make_async_copy(mixer.at[p], mixer_hbm.at[p], mixer_sems.at[p])

    def pair(p):
        slot = lax.rem(p, 2)

        @pl.when(p >= 2)
        def _():
            for store in stores(p - 2, slot):
                store.wait()

        keep_mixer(p).start()
        weight = mixer[pl.ds(p, 1)].reshape(width, 384)
        at = [pl.ds(pl.multiple_of(part * width + p * 128, 128), 128) for part in range(3)]
        bias = jnp.concatenate([mb_ref[:, columns] for columns in at], axis=1)
        mixed[pl.ds(slot, 1)] = (dot_nn(norm[...], weight) + bias).astype(BF16)[None]
        here = mixed.at[slot]
        q2 = here[:, 0:128] * jnp.asarray(0.125, BF16)
        start = start_row(len_ref, count, length)
        fwd_pair(
            q2, here.at[:, 128:256], here.at[:, 256:384], pre_ref[:, at[0]], pre_ref[:, at[1]],
            start, prefix, most, att.at[:, pl.ds(pl.multiple_of(p * 128, 128), 128)], lse_ref.at[p],
        )
        for store in stores(p, slot):
            store.start()

    def output_weight():
        return jnp.concatenate([wo[n].reshape(-1, wo.shape[5], width) for n in range(2)], axis=1).reshape(width, width)

    def second_norm():
        for p in (pairs - 2, pairs - 1):
            for store in stores(p, p % 2):
                store.wait()

        @pl.loop(0, tiles)
        def _(i):
            rows = rows_of(i)
            value = x[rows, :].astype(F32) + (dot_nn(att[rows, :], output_weight()) + bo_ref[...])
            mid[rows, :] = value
            hat, _ = norm_parts(value)
            norm[rows, :] = (hat * gain_ref[1:2, :] + shift_ref[1:2, :]).astype(BF16)
            acc[rows, :] = jnp.zeros((TILE, width), F32)
            gacc[rows, :] = jnp.zeros((TILE, width), F32)

    def chunk(j):
        e = ew.at[j]
        c = cw.at[j]
        bias = be_ref[pl.ds(j, 1), :]

        @pl.loop(0, tiles)
        def _(i):
            rows = rows_of(i)
            ev = e[...].reshape(width, -1)
            cv = c[...].reshape(-1, width)
            active, slope = gelu_both(dot_nn(norm[rows, :], ev) + bias)
            grad = (dot_nt(cot[rows, :], cv) * slope).astype(BF16)
            acc[rows, :] += dot_nn(active.astype(BF16), cv)
            gacc[rows, :] += dot_nt(grad, ev)

    @pl.loop(0, FF_TICK + chunks)
    def _(t):
        gather.tick(t)
        pl.when(t == 0)(first_norm)
        pl.when(t == 1)(prefix_rows)
        p = t - PAIR_TICK

        @pl.when((p >= 0) & (p < pairs))
        def _():
            pair(p)

        pl.when(t == PAIR_TICK + pairs)(second_norm)
        j = t - FF_TICK

        @pl.when(j >= 0)
        def _():
            chunk(j)

    def results(i):
        rows = rows_of(i)
        return [
            pltpu.make_async_copy(src.at[rows, :], dst.at[rows, :], out_sems.at[n, i])
            for n, (src, dst) in enumerate(((x, out_hbm), (gacc, gm_hbm), (att, ga_hbm)))
        ]

    @pl.loop(0, tiles)
    def _(i):
        rows = rows_of(i)
        value = mid[rows, :]
        x[rows, :] = (value + (acc[rows, :] + bc_ref[...])).astype(BF16)
        hat, rate = norm_parts(value)
        grad = cot[rows, :].astype(F32) + norm_back(hat, rate, gacc[rows, :], gain_ref[1:2, :])
        gacc[rows, :] = grad
        att[rows, :] = dot_nt(grad.astype(BF16), output_weight()).astype(BF16)
        for result in results(i):
            result.start()

    gather.finish()

    @pl.loop(0, pairs)
    def _(p):
        keep_mixer(p).wait()

    @pl.loop(0, tiles)
    def _(i):
        for result in results(i):
            result.wait()


def layer(dims, x, lengths, cot, m_shard, w_shard, e_shard, c_shard, reparam_in, reparam_out, embed, reparam_in_bias,
          reparam_out_bias, mixer_bias, output_bias, expand_bias, contract_bias, gains, shifts, prefix, most):
    length, width = x.shape
    pairs, chunks = m_shard.shape[0], e_shard.shape[0]
    rep = reparam_in.shape[1]
    anyspace = pl.BlockSpec(memory_space=pl.ANY)
    vmem = pl.BlockSpec(memory_space=pltpu.VMEM)
    dma = pltpu.SemaphoreType.DMA
    shape = jax.ShapeDtypeStruct
    held = lambda shard: (shard.shape[0],) + dims + shard.shape[1:]
    full = lambda kind: pltpu.VMEM((length, width), kind)
    return pl.pallas_call(
        functools.partial(layer_kernel, dims, prefix, most, lengths.shape[1]),
        in_specs=[pl.BlockSpec(memory_space=pltpu.SMEM)] + [anyspace] * 8 + [vmem] * 9,
        out_specs=[anyspace, anyspace, vmem, vmem, vmem] + [anyspace] * 4,
        out_shape=[
            shape((pairs, length, 384), BF16), shape((length, width), BF16), shape((pairs, 2, length), F32),
            shape((PAD, 2 * width), BF16), shape((PAD, rep), F32), shape(held(m_shard), BF16),
            shape((length, width), BF16), shape((length, width), F32), shape((length, width), BF16),
        ],
        scratch_shapes=[
            full(BF16), full(BF16), pltpu.VMEM(held(m_shard), BF16), pltpu.VMEM((2, length, 384), BF16), full(BF16),
            full(BF16), pltpu.VMEM(held(w_shard), BF16), full(F32), full(F32), full(F32),
            pltpu.VMEM(held(e_shard), BF16), pltpu.VMEM(held(c_shard), BF16),
            *gather_sems(pairs // 2), *gather_sems(pairs // 2), *gather_sems(1), *gather_sems(1),
            *gather_sems(chunks), *gather_sems(chunks),
            dma((5,)), dma((2,)), dma((2,)), dma((pairs,)), dma((3, length // TILE)),
        ],
        compiler_params=pltpu.CompilerParams(collective_id=0, has_side_effects=True, vmem_limit_bytes=60 << 20),
        name="layer",
    )(lengths, x, cot, m_shard, w_shard, e_shard, c_shard, reparam_in, reparam_out, embed, reparam_in_bias,
      reparam_out_bias, mixer_bias, output_bias, expand_bias, contract_bias, gains, shifts)


def back_kernel(dims, prefix, most, count, len_ref, mixed_ref, pk_ref, pv_ref, do_ref, o_ref, lse_ref,
                gain_ref, w_hbm, x_hbm, gm_hbm, gx_hbm, total_ref,
                dk_acc, dv_acc, dpk, dpv, gmix, w, x, gm, tiles, inbox, sums,
                in_sems, out_sems, give_send, give_recv, tell_send, tell_recv):
    length, width = x.shape
    q_ref, k_ref, v_ref = (mixed_ref.at[0, :, part * 128:(part + 1) * 128] for part in range(3))
    pair = pl.program_id(0)
    pairs = width // 128
    devices = math.prod(dims)
    narrow_size = dims[2] * dims[3]
    me = lax.axis_index("wide") * narrow_size + lax.axis_index("narrow")
    tile_count = 4 * pairs
    ratio = devices // tile_count
    owns = lax.rem(me, ratio) == 0
    own_tile = me // ratio
    place = lambda device: (device // narrow_size, lax.rem(device, narrow_size))
    loads = [
        pltpu.make_async_copy(src, dst, in_sems.at[n])
        for n, (src, dst) in enumerate(((x_hbm, x), (gm_hbm, gm)))
    ] + [
        pltpu.make_async_copy(w_hbm.at[n], w.at[:, n * 384:(n + 1) * 384], in_sems.at[2 + n]) for n in range(pairs)
    ]
    barrier = pltpu.get_barrier_semaphore()

    @pl.when(pair == 0)
    def _():
        for load in loads:
            load.start()

        @pl.loop(1, devices)
        def _(step):
            peer = place(lax.rem(me + step, devices))
            pl.semaphore_signal(barrier, inc=1, device_id=peer, device_id_type=MESH)

    start = start_row(len_ref, count, length)
    lane = lax.broadcasted_iota(jnp.int32, (1, 128), 1)
    pre_seen = lax.broadcasted_iota(jnp.int32, (PAD, BLOCK), 0) < prefix
    pk, pv = pk_ref[...], pv_ref[...]
    k_t = k_ref[...].T
    pk_t = pk.T
    head_of = lax.broadcasted_iota(jnp.int32, (8, 128), 0)
    pick = ((lax.broadcasted_iota(jnp.int32, (8, 128), 1) // 64) == head_of).astype(F32).astype(BF16)
    columns = [pl.ds(pl.multiple_of(pair * 384 + part * 128, 128), 128) for part in range(3)]
    for qi in range(length // BLOCK):
        rows = slice(qi * BLOCK, (qi + 1) * BLOCK)
        lo = span(qi, most)
        st = start[:, rows]
        q2 = q_ref[rows, :] * jnp.asarray(0.125, BF16)
        do2 = do_ref[rows, :]
        prod = do2.astype(F32) * o_ref[rows, :].astype(F32)
        high = prod.astype(BF16)
        low = (prod - high.astype(F32)).astype(BF16)
        delta2 = dot_nt(pick, high) + dot_nt(pick, low)
        halves = []
        for h in range(2):
            mine = (lane // 64) == h
            qh = jnp.where(mine, q2, jnp.zeros((), BF16))
            doh = jnp.where(mine, do2, jnp.zeros((), BF16))
            lse = lse_ref[0, h:h + 1, rows]
            delta = delta2[h:h + 1]
            p = jnp.where(pre_seen, jnp.exp(dot_nt(pk, qh) - lse), 0.0)
            ds = (p * (dot_nt(pv, doh) - delta)).astype(BF16)
            one_dpk = dot_nn(ds, qh)
            one_dpv = dot_nn(p.astype(BF16), doh)
            if qi == 0 and h == 0:
                dpk[...], dpv[...] = one_dpk, one_dpv
            else:
                dpk[...] += one_dpk
                dpv[...] += one_dpv
            dq = dot_nn(pk_t[h * 64:(h + 1) * 64], ds)
            for kj in range(lo, qi + 1):
                keys = slice(kj * BLOCK, (kj + 1) * BLOCK)
                s = dot_nt(k_ref[keys, :], qh)
                p = jnp.exp(s - lse)
                p = jnp.where(visible(st, kj * BLOCK, BLOCK, qi * BLOCK, BLOCK, kj == qi), p, 0.0)
                dp = dot_nt(v_ref[keys, :], doh)
                ds = (p * (dp - delta)).astype(BF16)
                dv = dot_nn(p.astype(BF16), doh)
                dk = dot_nn(ds, qh)
                if kj == qi and h == 0:
                    dv_acc[keys, :], dk_acc[keys, :] = dv, dk
                else:
                    dv_acc[keys, :] += dv
                    dk_acc[keys, :] += dk
                dq = dq + dot_nn(k_t[h * 64:(h + 1) * 64, keys], ds)
            halves.append(dq * 0.125)
        gmix[rows, columns[0]] = jnp.concatenate(halves, axis=0).T.astype(BF16)
    gmix[:, columns[1]] = dk_acc[...].astype(BF16)
    gmix[:, columns[2]] = dv_acc[...].astype(BF16)

    def give(part):
        tile = part * pairs + pair
        return pltpu.make_async_remote_copy(
            src_ref=tiles.at[tile], dst_ref=inbox.at[me], send_sem=give_send, recv_sem=give_recv,
            device_id=place(tile * ratio), device_id_type=MESH,
        )

    @pl.when(pair == 0)
    def _():
        pl.semaphore_wait(barrier, devices - 1)

    for part, (ref, half) in enumerate(((dpk, 0), (dpk, 1), (dpv, 0), (dpv, 1))):
        value = ref[half * 8:(half + 1) * 8, :]
        tile = part * pairs + pair
        tiles[pl.ds(tile, 1)] = value[None]
        to_me = owns & (tile == own_tile)

        @pl.when(to_me)
        def _():
            inbox[pl.ds(me, 1)] = value[None]

        @pl.when(jnp.logical_not(to_me))
        def _():
            give(part).start()

    @pl.when(pair == pairs - 1)
    def _():
        for load in loads:
            load.wait()
        tall = 256

        def store(i):
            rows = pl.ds(i * tall, tall)
            return pltpu.make_async_copy(x.at[rows, :], gx_hbm.at[rows, :], out_sems.at[i])

        def finish_rows(i):
            rows = pl.ds(i * tall, tall)
            grad = dot_nt(gmix[rows, :], w[...])
            hat, rate = norm_parts(x[rows, :].astype(F32))
            x[rows, :] = (gm[rows, :] + norm_back(hat, rate, grad, gain_ref[...])).astype(BF16)
            store(i).start()

        def bytes_of(ref, n, send, recv):
            part = ref.at[pl.ds(0, n)]
            return pltpu.make_async_remote_copy(
                src_ref=part, dst_ref=part, send_sem=send, recv_sem=recv,
                device_id=place(lax.rem(me + 1, devices)), device_id_type=MESH,
            )

        finish_rows(0)
        finish_rows(1)

        @pl.when(owns)
        def _():
            bytes_of(inbox, devices - 1, give_send, give_recv).wait_recv()
            summed = inbox[0]
            for device in range(1, devices):
                summed = summed + inbox[device]
            sums[pl.ds(own_tile, 1)] = summed[None]

            @pl.loop(1, devices)
            def _(step):
                pltpu.make_async_remote_copy(
                    src_ref=sums.at[own_tile], dst_ref=sums.at[own_tile], send_sem=tell_send,
                    recv_sem=tell_recv, device_id=place(lax.rem(me + step, devices)), device_id_type=MESH,
                ).start()

        finish_rows(2)
        finish_rows(3)

        @pl.when(owns)
        def _():
            bytes_of(tiles, tile_count - 1, give_send, give_recv).wait_send()
            bytes_of(inbox, devices - 1, tell_send, tell_recv).wait_send()
            bytes_of(tiles, tile_count - 1, tell_send, tell_recv).wait_recv()

        @pl.when(jnp.logical_not(owns))
        def _():
            bytes_of(tiles, tile_count, give_send, give_recv).wait_send()
            bytes_of(tiles, tile_count, tell_send, tell_recv).wait_recv()

        total_ref[...] = sums[...]
        for i in range(length // tall):
            store(i).wait()


def attend_back(dims, mixed, lengths, pre, grad, attended, lse, gain, full_mixer, x, grad_middle, prefix, most):
    length, width = grad.shape
    pairs = width // 128
    count = lengths.shape[1]
    devices = math.prod(dims)
    col = lambda off: pl.BlockSpec((length, 128), lambda p: (0, p + off))
    pcol = lambda off: pl.BlockSpec((PAD, 128), lambda p: (0, p + off))
    anyspace = pl.BlockSpec(memory_space=pl.ANY)
    dma = pltpu.SemaphoreType.DMA
    return pl.pallas_call(
        functools.partial(back_kernel, dims, prefix, most, count),
        grid=(pairs,),
        in_specs=[pl.BlockSpec(memory_space=pltpu.SMEM), pl.BlockSpec((1, length, 384), lambda p: (p, 0, 0)),
                  pcol(0), pcol(pairs), col(0), col(0), pl.BlockSpec((1, 2, length), lambda p: (p, 0, 0)),
                  pl.BlockSpec((1, width), lambda p: (0, 0)), anyspace, anyspace, anyspace],
        out_specs=[anyspace, pl.BlockSpec((4 * pairs, 8, 128), lambda p: (0, 0, 0))],
        out_shape=[jax.ShapeDtypeStruct((length, width), BF16), jax.ShapeDtypeStruct((4 * pairs, 8, 128), F32)],
        scratch_shapes=[pltpu.VMEM((length, 128), F32)] * 2 + [pltpu.VMEM((PAD, 128), F32)] * 2 + [
            pltpu.VMEM((length, 3 * width), BF16), pltpu.VMEM((width, 3 * width), BF16),
            pltpu.VMEM((length, width), BF16), pltpu.VMEM((length, width), F32),
            pltpu.VMEM((4 * pairs, 8, 128), F32), pltpu.VMEM((devices, 8, 128), F32),
            pltpu.VMEM((4 * pairs, 8, 128), F32),
            dma((2 + pairs,)), dma((length // 256,)), dma(()), dma(()), dma(()), dma(()),
        ],
        compiler_params=pltpu.CompilerParams(collective_id=2, has_side_effects=True, vmem_limit_bytes=56 << 20),
        name="attend_back",
    )(lengths, mixed, pre, pre, grad, attended, lse, gain, full_mixer, x, grad_middle)


def reparam_kernel(prefix, total_ref, sq_ref, embed_ref, ro_ref, ri_ref, gx_hbm, out_hbm,
                   gx_out, out_out, ge_ref, gi_ref, gib_ref, go_ref, gob_ref, gs, sems):
    step = pl.program_id(0)
    steps = pl.num_programs(0)
    pairs = total_ref.shape[0] // 4
    moves = [pltpu.make_async_copy(gx_hbm, gx_out, sems.at[0]), pltpu.make_async_copy(out_hbm, out_out, sems.at[1])]

    @pl.when(step == 0)
    def _():
        for move in moves:
            move.start()
        gs[...] = jnp.zeros_like(gs)

    per = 2 * pairs // steps
    blocks = []
    for n in range(per):
        block = step * per + n
        part, pair = block // pairs, lax.rem(block, pairs)
        top = total_ref[pl.ds(2 * part * pairs + pair, 1)][0]
        low = total_ref[pl.ds((2 * part + 1) * pairs + pair, 1)][0]
        blocks.append(jnp.concatenate([top, low], axis=0))
    grad = jnp.concatenate(blocks, axis=1)
    go_ref[...] = dot_fine(sq_ref[...], grad, ((0,), (0,)))
    gob_ref[...] = jnp.sum(grad, axis=0, keepdims=True)
    gs[...] += dot_fine(grad, ro_ref[...], ((1,), (1,)))

    @pl.when(step == steps - 1)
    def _():
        squashed = sq_ref[...]
        inner = gs[...] * (1.0 - squashed * squashed)
        gi_ref[...] = dot_fine(embed_ref[...], inner, ((0,), (0,)))
        gib_ref[...] = jnp.sum(inner, axis=0, keepdims=True)
        ge_ref[...] = dot_fine(inner, ri_ref[...], ((1,), (1,)))[:prefix]
        for move in moves:
            move.wait()


def reparam_back(total, squashed, embed, reparam_out, reparam_in, grad_tokens, out_tokens, prefix):
    width2 = reparam_out.shape[1]
    rep = reparam_out.shape[0]
    width = embed.shape[1]
    steps = 4
    whole = lambda array: pl.BlockSpec(array.shape, lambda i: (0,) * array.ndim)
    anyspace = pl.BlockSpec(memory_space=pl.ANY)
    shape = jax.ShapeDtypeStruct
    return pl.pallas_call(
        functools.partial(reparam_kernel, prefix),
        grid=(steps,),
        in_specs=[whole(total), whole(squashed), whole(embed), pl.BlockSpec((rep, width2 // steps), lambda i: (0, i)),
                  whole(reparam_in), anyspace, anyspace],
        out_specs=[anyspace, anyspace,
                   pl.BlockSpec((prefix, width), lambda i: (0, 0)), pl.BlockSpec((width, rep), lambda i: (0, 0)),
                   pl.BlockSpec((1, rep), lambda i: (0, 0)), pl.BlockSpec((rep, width2 // steps), lambda i: (0, i)),
                   pl.BlockSpec((1, width2 // steps), lambda i: (0, i))],
        out_shape=[shape(grad_tokens.shape, BF16), shape(out_tokens.shape, BF16), shape((prefix, width), F32),
                   shape((width, rep), F32), shape((1, rep), F32), shape((rep, width2), F32), shape((1, width2), F32)],
        scratch_shapes=[pltpu.VMEM(squashed.shape, F32), pltpu.SemaphoreType.DMA((2,))],
        compiler_params=pltpu.CompilerParams(vmem_limit_bytes=40 << 20),
        name="reparam_back",
    )(total, squashed, embed, reparam_out, reparam_in, grad_tokens, out_tokens)


def shards(
    dims,
    tokens,
    lengths,
    cotangent,
    mixer_weight,
    output_weight,
    expand_weight,
    contract_weight,
    mixer_bias,
    output_bias,
    expand_bias,
    contract_bias,
    norm_gains,
    norm_shifts,
    prefix_embed,
    reparam_in,
    reparam_in_bias,
    reparam_out,
    reparam_out_bias,
):
    row_count, length, model_width = tokens.shape
    total_rows = row_count * length
    devices = math.prod(dims)
    hidden = expand_weight.shape[1]
    part = hidden // devices // CHUNKS
    by_chunk = lambda array: array.reshape(-1, devices, CHUNKS, part).transpose(2, 0, 1, 3).reshape(CHUNKS, -1, devices * part)
    expand_parts = by_chunk(expand_weight)
    expand_bias_parts = by_chunk(expand_bias)[:, 0]
    contract_parts = contract_weight.reshape(CHUNKS, part, model_width)
    prefix_count = prefix_embed.shape[0]
    tall = lambda array: jnp.pad(array, ((0, PAD - prefix_count), (0, 0)))
    rows = mixer_weight.shape[0]
    pairs = model_width // 128
    mixer_parts = mixer_weight.reshape(rows, 3, pairs, 128).transpose(2, 0, 1, 3).reshape(pairs, rows, 384)
    x = tokens.reshape(total_rows, model_width)
    as_row = lambda array: array.reshape(1, -1)
    embed = tall(prefix_embed)
    mixed, attended, log_sums, pre, squashed, full_mixer, out_tokens, grad_middle, grad_attended = layer(
        dims, x, lengths, cotangent.reshape(total_rows, model_width), mixer_parts,
        output_weight.reshape(2, rows // 2, model_width), expand_parts, contract_parts, reparam_in, reparam_out, embed,
        as_row(reparam_in_bias), as_row(reparam_out_bias), as_row(mixer_bias), as_row(output_bias), expand_bias_parts,
        as_row(contract_bias), norm_gains, norm_shifts, prefix_count, MOST,
    )
    grad_tokens, total = attend_back(
        dims, mixed, lengths, pre, grad_attended, attended, log_sums, norm_gains[0:1],
        full_mixer.reshape(pairs, model_width, 384), x, grad_middle, prefix_count, MOST,
    )
    grad_tokens, out_tokens, grad_embed, grad_in, grad_in_bias, grad_out, grad_out_bias = reparam_back(
        total, squashed, embed, reparam_out, reparam_in, grad_tokens, out_tokens, prefix_count
    )
    return (
        out_tokens.reshape(tokens.shape), grad_tokens.reshape(tokens.shape), grad_embed, grad_in, grad_in_bias[0],
        grad_out, grad_out_bias[0],
    )


def solution(mesh):
    return jax.shard_map(
        functools.partial(shards, grid_dims(mesh.shape)),
        mesh=mesh,
        in_specs=(
            P(("wide", "narrow"), None, None),
            P(("wide", "narrow"), None),
            P(("wide", "narrow"), None, None),
            P(("wide", "narrow"), None),
            P(("wide", "narrow"), None),
            P(("wide", "narrow"), None),
            P(("wide", "narrow"), None),
            P(),
            P(),
            P(),
            P(),
            P(),
            P(),
            P(),
            P(),
            P(),
            P(),
            P(),
        ),
        out_specs=(
            P(("wide", "narrow"), None, None),
            P(("wide", "narrow"), None, None),
            P(),
            P(),
            P(),
            P(),
            P(),
        ),
        check_vma=False,
    )
```

```python
import functools
import math

import jax
import jax.numpy as jnp
from jax import lax
from jax.experimental import pallas as pl
from jax.experimental.pallas import tpu as pltpu
from jax.sharding import PartitionSpec as P

MOST = 512


BLOCK = 256
PAD = 16
F32, BF16 = jnp.float32, jnp.bfloat16


def dot_nt(a, b):
    return lax.dot_general(a, b, (((1,), (1,)), ((), ())), preferred_element_type=F32)


def dot_nn(a, b):
    return lax.dot_general(a, b, (((1,), (0,)), ((), ())), preferred_element_type=F32)


def start_row(lengths_ref, count, length):
    place = lax.broadcasted_iota(jnp.int32, (1, length), 1)
    start = jnp.zeros((1, length), jnp.int32)
    total = jnp.int32(0)
    for j in range(count):
        total = total + lengths_ref[0, j]
        start = jnp.where(place >= total, total, start)
    return start


def visible(start, first_key, keys, first_query, queries, diagonal):
    key = lax.broadcasted_iota(jnp.int32, (keys, queries), 0) + first_key
    seen = key >= start
    if diagonal:
        query = lax.broadcasted_iota(jnp.int32, (keys, queries), 1) + first_query
        seen = seen & (key <= query)
    return seen


def span(qi, most):
    return max(0, qi - most // BLOCK)


def fwd_pair(q_ref, k_ref, v_ref, pk, pv, start, prefix, most, o_ref, lse_ref, blocks):
    lane = lax.broadcasted_iota(jnp.int32, (1, 128), 1)
    pre_seen = lax.broadcasted_iota(jnp.int32, (PAD, BLOCK), 0) < prefix
    v_t = v_ref[:(max(blocks) + 1) * BLOCK, :].T
    pv_t = pv.T
    for qi in blocks:
        rows = slice(qi * BLOCK, (qi + 1) * BLOCK)
        lo = span(qi, most)
        st = start[:, rows]
        q2 = q_ref[rows, :] * jnp.asarray(0.125, BF16)
        halves = []
        for h in range(2):
            qh = jnp.where((lane // 64) == h, q2, jnp.zeros((), BF16))
            s_pre = jnp.where(pre_seen, dot_nt(pk, qh), -1e30)
            peak = jnp.max(s_pre, axis=0, keepdims=True)
            parts = []
            for kj in range(lo, qi + 1):
                s = dot_nt(k_ref[kj * BLOCK:(kj + 1) * BLOCK, :], qh)
                s = jnp.where(visible(st, kj * BLOCK, BLOCK, qi * BLOCK, BLOCK, kj == qi), s, -1e30)
                peak = jnp.maximum(peak, jnp.max(s, axis=0, keepdims=True))
                parts.append(s)
            p = jnp.exp(s_pre - peak)
            total = jnp.sum(p, axis=0, keepdims=True)
            o = dot_nn(pv_t[h * 64:(h + 1) * 64], p.astype(BF16))
            for n, kj in enumerate(range(lo, qi + 1)):
                p = jnp.exp(parts[n] - peak)
                total = total + jnp.sum(p, axis=0, keepdims=True)
                o = o + dot_nn(v_t[h * 64:(h + 1) * 64, kj * BLOCK:(kj + 1) * BLOCK], p.astype(BF16))
            halves.append(o / total)
            lse_ref[h:h + 1, rows] = peak + jnp.log(total)
        o_ref[rows, :] = jnp.concatenate(halves, axis=0).T.astype(BF16)


CHUNKS = 8
TILE = 256
MESH = pl.DeviceIdType.MESH
XY, YX = (0, 1, 2, 3), (0, 2, 1, 3)


def grid_dims(mesh_shape):
    wide, narrow = mesh_shape["wide"], mesh_shape["narrow"]
    return (wide // 2, 2, narrow // 2, 2)


class Family:
    def __init__(self, source, target, order, sems, part=()):
        self.source, self.target, self.order, self.part = source, target, order, part
        self.send, self.recv, self.own = sems


class Group:
    def __init__(self, families, offset, lag, ahead):
        self.families, self.offset, self.lag, self.ahead = families, offset, lag, ahead
        self.count = families[0].source.shape[0]

    def tick(self, stage):
        return self.offset + (self.lag * stage if stage >= 0 else -self.ahead)


class Gather:
    def __init__(self, dims, groups):
        self.dims = dims
        wide, narrow = lax.axis_index("wide"), lax.axis_index("narrow")
        self.at = (wide // dims[1], lax.rem(wide, dims[1]), narrow // dims[3], lax.rem(narrow, dims[3]))
        self.groups = groups
        self.peers = [
            [self.device(dim, lax.rem(self.at[dim] + step, size)) for step in range(1, size)]
            for dim, size in enumerate(dims)
        ]

    def device(self, dim, index):
        at = list(self.at)
        at[dim] = index
        return (at[0] * self.dims[1] + at[1], at[2] * self.dims[3] + at[3])

    def greet(self):
        barrier = pltpu.get_barrier_semaphore()
        for peers in self.peers:
            for peer in peers:
                pl.semaphore_signal(barrier, inc=1, device_id=peer, device_id_type=MESH)
        pl.semaphore_wait(barrier, sum(len(peers) for peers in self.peers))

    def view(self, family, j, stage, index):
        done, dim = family.order[:stage], family.order[stage]
        return family.target.at[
            (j,)
            + tuple(slice(None) if d in done else (index if d == dim else self.at[d]) for d in range(4))
            + family.part
        ]

    def keep(self, family, j):
        return pltpu.make_async_copy(
            family.source.at[(j,) + family.part], family.target.at[(j,) + self.at + family.part], family.own.at[j]
        )

    def start(self, family, j, stage):
        dim = family.order[stage]
        if stage == 0:
            self.keep(family, j).start()
        mine = self.view(family, j, stage, self.at[dim])
        for peer in self.peers[dim]:
            pltpu.make_async_remote_copy(
                src_ref=family.source.at[(j,) + family.part] if stage == 0 else mine,
                dst_ref=mine,
                send_sem=family.send.at[j, stage],
                recv_sem=family.recv.at[j, stage],
                device_id=peer,
                device_id_type=MESH,
            ).start()

    def whole(self, family, j, stage):
        dim = family.order[stage]
        part = self.view(family, j, stage, pl.ds(0, self.dims[dim] - 1))
        return pltpu.make_async_remote_copy(
            src_ref=part, dst_ref=part, send_sem=family.send.at[j, stage], recv_sem=family.recv.at[j, stage],
            device_id=self.peers[dim][0], device_id_type=MESH,
        )

    def arrive(self, family, j, stage):
        if stage == 0:
            self.keep(family, j).wait()
        self.whole(family, j, stage).wait_recv()

    def begin(self):
        for group in self.groups:
            for j in range(group.count):
                if group.tick(-1) + 2 * j < 0:
                    for family in group.families:
                        self.start(family, j, 0)

    def tick(self, double, half):
        for stage in (3, 2, 1, 0, -1):
            for group in self.groups:
                past = half - group.tick(stage)
                if past % 2:
                    continue
                j = double + past // 2

                @pl.when((j >= 0) & (j < group.count))
                def _():
                    for family in group.families:
                        if stage >= 0:
                            self.arrive(family, j, stage)
                        if stage < 3:
                            self.start(family, j, stage + 1)

    def finish(self):
        for group in self.groups:

            @pl.loop(0, group.count)
            def _(j):
                for family in group.families:
                    for stage in range(4):
                        self.whole(family, j, stage).wait_send()


def gather_sems(count):
    dma = pltpu.SemaphoreType.DMA
    return [dma((count, 4)), dma((count, 4)), dma((count,))]


def norm_parts(values):
    center = values - jnp.mean(values, axis=-1, keepdims=True)
    rate = lax.rsqrt(jnp.mean(center * center, axis=-1, keepdims=True) + 1e-05)
    return center * rate, rate


def norm_back(hat, rate, grad, gain):
    inner = grad * gain
    return rate * (
        inner - jnp.mean(inner, axis=-1, keepdims=True) - hat * jnp.mean(inner * hat, axis=-1, keepdims=True)
    )


def split(value):
    high = value.astype(BF16)
    return high, (value - high.astype(F32)).astype(BF16)


def dot_fine(left, right, dims):
    lh, ll = split(left)
    rh, rl = split(right)
    one = lambda a, b: lax.dot_general(a, b, (dims, ((), ())), preferred_element_type=F32)
    return one(lh, rh) + (one(lh, rl) + one(ll, rh))


ROOT = math.sqrt(2.0 / math.pi)


def gelu_both(v):
    square = v * v
    th = jnp.tanh(ROOT * v * (1.0 + 0.044715 * square))
    half = 0.5 * (1.0 + th)
    slope = half + 0.5 * v * (1.0 - th * th) * (ROOT * (1.0 + 3 * 0.044715 * square))
    return v * half, slope


M_LAG = 3
PAIR_TICK = 9
MID_TICK = 25
FF_TICK = 27
FF_LAG = 3
W_TICK = 12
AHEAD = 5


def layer_kernel(dims, prefix, most, count, len_ref, x_hbm, cot_hbm, m_hbm, w_hbm, e_hbm, c_hbm, ri_hbm, ro_hbm,
                 embed_ref, rib_ref, rob_ref, mb_ref, bo_ref, be_ref, bc_ref, gain_ref, shift_ref,
                 mixed_hbm, att_hbm, lse_ref, pre_ref, sq_ref, mixer_hbm, out_hbm, gm_hbm, ga_hbm,
                 x, norm, mixer, mixed, att, cot, wo, mid, acc, gacc, ew, cw,
                 m0_send, m0_recv, m0_own, m1_send, m1_recv, m1_own, w0_send, w0_recv, w0_own, w1_send, w1_recv, w1_own,
                 e_send, e_recv, e_own, c_send, c_recv, c_own,
                 in_sems, mixed_sems, att_sems, mixer_sems, out_sems):
    length, width = x.shape
    pairs, chunks = m_hbm.shape[0], e_hbm.shape[0]
    rep = sq_ref.shape[1]
    both = lambda rows: [(order, (pl.ds(n * rows // 2, rows // 2),)) for n, order in enumerate((XY, YX))]
    m_sems = ((m0_send, m0_recv, m0_own), (m1_send, m1_recv, m1_own))
    w_sems = ((w0_send, w0_recv, w0_own), (w1_send, w1_recv, w1_own))
    halves = lambda rows: [(order, (pl.ds(n * rows // 2, rows // 2),)) for n, order in enumerate((XY, YX))]
    m_sems = ((m0_send, m0_recv, m0_own), (m1_send, m1_recv, m1_own))
    w_sems = ((w0_send, w0_recv, w0_own), (w1_send, w1_recv, w1_own))
    gather = Gather(dims, [
        Group([Family(m_hbm, mixer, order, m_sems[n], part) for n, (order, part) in enumerate(halves(m_hbm.shape[1]))],
              0, M_LAG, AHEAD),
        Group([Family(w_hbm, wo, order, w_sems[n], part) for n, (order, part) in enumerate(halves(w_hbm.shape[1]))],
              W_TICK, 2, AHEAD),
        Group([Family(e_hbm, ew, XY, (e_send, e_recv, e_own)), Family(c_hbm, cw, YX, (c_send, c_recv, c_own))],
              FF_TICK - 3 * FF_LAG, FF_LAG, AHEAD),
    ])
    loads = [
        pltpu.make_async_copy(src, dst, in_sems.at[n])
        for n, (src, dst) in enumerate((
            (x_hbm, x), (ri_hbm, mid.at[:, :rep]), (ro_hbm.at[:, :width], acc.at[:rep]), (ro_hbm.at[:, width:], gacc.at[:rep]),
            (cot_hbm, cot),
        ))
    ]
    for load in loads:
        load.start()
    gather.greet()
    gather.begin()
    tiles = length // TILE

    def rows_of(i):
        return pl.ds(pl.multiple_of(i * TILE, TILE), TILE)

    def first_norm():
        loads[0].wait()

        @pl.loop(0, tiles)
        def _(i):
            rows = rows_of(i)
            hat, _ = norm_parts(x[rows, :].astype(F32))
            norm[rows, :] = (hat * gain_ref[0:1, :] + shift_ref[0:1, :]).astype(BF16)

    def prefix_rows():
        for load in loads[1:]:
            load.wait()
        seen = lax.broadcasted_iota(jnp.int32, (PAD, 1), 0) < prefix
        squashed = jnp.where(seen, jnp.tanh(dot_fine(embed_ref[...], mid[:, :rep], ((1,), (0,))) + rib_ref[...]), 0.0)
        sq_ref[...] = squashed
        for part, ref in enumerate((acc, gacc)):
            columns = slice(part * width, (part + 1) * width)
            whole = dot_fine(squashed, ref[:rep, :], ((1,), (0,))) + rob_ref[:, columns]
            pre_ref[:, columns] = jnp.where(seen, whole, 0.0).astype(BF16)

    def stores(p, slot):
        columns = pl.ds(pl.multiple_of(p * 128, 128), 128)
        return [
            pltpu.make_async_copy(mixed.at[slot], mixed_hbm.at[p], mixed_sems.at[slot]),
            pltpu.make_async_copy(att.at[:, columns], att_hbm.at[:, columns], att_sems.at[slot]),
        ]

    def keep_mixer(p):
        return pltpu.make_async_copy(mixer.at[p], mixer_hbm.at[p], mixer_sems.at[p])

    def pair(p, part):
        slot = lax.rem(p, 2)
        at = [pl.ds(pl.multiple_of(third * width + p * 128, 128), 128) for third in range(3)]
        here = mixed.at[slot]

        if part == 0:

            @pl.when(p >= 2)
            def _():
                for store in stores(p - 2, slot):
                    store.wait()

            keep_mixer(p).start()
            weight = mixer[pl.ds(p, 1)].reshape(width, 384)
            bias = jnp.concatenate([mb_ref[:, columns] for columns in at], axis=1)
            mixed[pl.ds(slot, 1)] = (dot_nn(norm[...], weight) + bias).astype(BF16)[None]
        blocks = length // BLOCK
        fwd_pair(
            here.at[:, 0:128], here.at[:, 128:256], here.at[:, 256:384], pre_ref[:, at[0]], pre_ref[:, at[1]],
            start_row(len_ref, count, length), prefix, most, att.at[:, at[0]], lse_ref.at[p],
            range(blocks // 2) if part == 0 else range(blocks // 2, blocks),
        )
        if part == 1:
            for store in stores(p, slot):
                store.start()

    def output_weight():
        return wo[0].reshape(width, width)

    def second_norm(part):
        if part == 0:
            for p in (pairs - 2, pairs - 1):
                for store in stores(p, p % 2):
                    store.wait()

        @pl.loop(part * tiles // 2, (part + 1) * tiles // 2)
        def _(i):
            rows = rows_of(i)
            value = x[rows, :].astype(F32) + (dot_nn(att[rows, :], output_weight()) + bo_ref[...])
            mid[rows, :] = value
            hat, _ = norm_parts(value)
            norm[rows, :] = (hat * gain_ref[1:2, :] + shift_ref[1:2, :]).astype(BF16)
            acc[rows, :] = jnp.zeros((TILE, width), F32)
            gacc[rows, :] = jnp.zeros((TILE, width), F32)

    def chunk(j, part):
        e = ew.at[j]
        c = cw.at[j]
        bias = be_ref[pl.ds(j, 1), :]

        @pl.loop(part * tiles // 2, (part + 1) * tiles // 2)
        def _(i):
            rows = rows_of(i)
            ev = e[...].reshape(width, -1)
            cv = c[...].reshape(-1, width)
            active, slope = gelu_both(dot_nn(norm[rows, :], ev) + bias)
            grad = (dot_nt(cot[rows, :], cv) * slope).astype(BF16)
            acc[rows, :] += dot_nn(active.astype(BF16), cv)
            gacc[rows, :] += dot_nt(grad, ev)

    @pl.loop(0, (FF_TICK + 2 * chunks + 1) // 2)
    def _(double):
        for half in range(2):
            gather.tick(double, half)
            if half == 0:
                pl.when(double == 0)(first_norm)
            else:
                pl.when(double == 0)(prefix_rows)
            part = (half - PAIR_TICK) % 2
            p = double + (half - PAIR_TICK) // 2

            @pl.when((p >= 0) & (p < pairs))
            def _():
                pair(p, part)

            part = (half - MID_TICK) % 2
            pl.when(double + (half - MID_TICK) // 2 == 0)(functools.partial(second_norm, part))
            part = (half - FF_TICK) % 2
            j = double + (half - FF_TICK) // 2

            @pl.when((j >= 0) & (j < chunks))
            def _():
                chunk(j, part)

    def results(i):
        rows = rows_of(i)
        return [
            pltpu.make_async_copy(src.at[rows, :], dst.at[rows, :], out_sems.at[n, i])
            for n, (src, dst) in enumerate(((x, out_hbm), (gacc, gm_hbm), (att, ga_hbm)))
        ]

    @pl.loop(0, tiles)
    def _(i):
        rows = rows_of(i)
        value = mid[rows, :]
        x[rows, :] = (value + (acc[rows, :] + bc_ref[...])).astype(BF16)
        hat, rate = norm_parts(value)
        grad = cot[rows, :].astype(F32) + norm_back(hat, rate, gacc[rows, :], gain_ref[1:2, :])
        gacc[rows, :] = grad
        att[rows, :] = dot_nt(grad.astype(BF16), output_weight()).astype(BF16)
        for result in results(i):
            result.start()

    gather.finish()

    @pl.loop(0, pairs)
    def _(p):
        keep_mixer(p).wait()

    @pl.loop(0, tiles)
    def _(i):
        for result in results(i):
            result.wait()


def layer(dims, x, lengths, cot, m_shard, w_shard, e_shard, c_shard, reparam_in, reparam_out, embed, reparam_in_bias,
          reparam_out_bias, mixer_bias, output_bias, expand_bias, contract_bias, gains, shifts, prefix, most):
    length, width = x.shape
    pairs, chunks = m_shard.shape[0], e_shard.shape[0]
    rep = reparam_in.shape[1]
    anyspace = pl.BlockSpec(memory_space=pl.ANY)
    vmem = pl.BlockSpec(memory_space=pltpu.VMEM)
    dma = pltpu.SemaphoreType.DMA
    shape = jax.ShapeDtypeStruct
    held = lambda shard: (shard.shape[0],) + dims + shard.shape[1:]
    full = lambda kind: pltpu.VMEM((length, width), kind)
    return pl.pallas_call(
        functools.partial(layer_kernel, dims, prefix, most, lengths.shape[1]),
        in_specs=[pl.BlockSpec(memory_space=pltpu.SMEM)] + [anyspace] * 8 + [vmem] * 9,
        out_specs=[anyspace, anyspace, vmem, vmem, vmem] + [anyspace] * 4,
        out_shape=[
            shape((pairs, length, 384), BF16), shape((length, width), BF16), shape((pairs, 2, length), F32),
            shape((PAD, 2 * width), BF16), shape((PAD, rep), F32), shape(held(m_shard), BF16),
            shape((length, width), BF16), shape((length, width), F32), shape((length, width), BF16),
        ],
        scratch_shapes=[
            full(BF16), full(BF16), pltpu.VMEM(held(m_shard), BF16), pltpu.VMEM((2, length, 384), BF16), full(BF16),
            full(BF16), pltpu.VMEM(held(w_shard), BF16), full(F32), full(F32), full(F32),
            pltpu.VMEM(held(e_shard), BF16), pltpu.VMEM(held(c_shard), BF16),
            *gather_sems(pairs), *gather_sems(pairs), *gather_sems(1), *gather_sems(1),
            *gather_sems(chunks), *gather_sems(chunks),
            dma((5,)), dma((2,)), dma((2,)), dma((pairs,)), dma((3, length // TILE)),
        ],
        compiler_params=pltpu.CompilerParams(collective_id=0, has_side_effects=True, vmem_limit_bytes=60 << 20),
        name="layer",
    )(lengths, x, cot, m_shard, w_shard, e_shard, c_shard, reparam_in, reparam_out, embed, reparam_in_bias,
      reparam_out_bias, mixer_bias, output_bias, expand_bias, contract_bias, gains, shifts)


def back_kernel(dims, prefix, most, count, len_ref, mixed_ref, pk_ref, pv_ref, do_ref, o_ref, lse_ref,
                gain_ref, w_hbm, x_hbm, gm_hbm, gx_hbm, total_ref,
                dk_acc, dv_acc, dpk, dpv, gmix, w, x, gm, tiles, inbox, sums,
                in_sems, out_sems, give_send, give_recv, tell_send, tell_recv):
    length, width = x.shape
    q_ref, k_ref, v_ref = (mixed_ref.at[0, :, part * 128:(part + 1) * 128] for part in range(3))
    pair = pl.program_id(0)
    pairs = width // 128
    devices = math.prod(dims)
    narrow_size = dims[2] * dims[3]
    me = lax.axis_index("wide") * narrow_size + lax.axis_index("narrow")
    tile_count = 4 * pairs
    ratio = devices // tile_count
    owns = lax.rem(me, ratio) == 0
    own_tile = me // ratio
    place = lambda device: (device // narrow_size, lax.rem(device, narrow_size))
    loads = [
        pltpu.make_async_copy(src, dst, in_sems.at[n])
        for n, (src, dst) in enumerate(((x_hbm, x), (gm_hbm, gm)))
    ] + [
        pltpu.make_async_copy(w_hbm.at[n], w.at[:, n * 384:(n + 1) * 384], in_sems.at[2 + n]) for n in range(pairs)
    ]
    barrier = pltpu.get_barrier_semaphore()

    @pl.when(pair == 0)
    def _():
        for load in loads:
            load.start()

        @pl.loop(1, devices)
        def _(step):
            peer = place(lax.rem(me + step, devices))
            pl.semaphore_signal(barrier, inc=1, device_id=peer, device_id_type=MESH)

    start = start_row(len_ref, count, length)
    lane = lax.broadcasted_iota(jnp.int32, (1, 128), 1)
    pre_seen = lax.broadcasted_iota(jnp.int32, (PAD, BLOCK), 0) < prefix
    pk, pv = pk_ref[...], pv_ref[...]
    k_t = k_ref[...].T
    pk_t = pk.T
    head_of = lax.broadcasted_iota(jnp.int32, (8, 128), 0)
    pick = ((lax.broadcasted_iota(jnp.int32, (8, 128), 1) // 64) == head_of).astype(F32).astype(BF16)
    columns = [pl.ds(pl.multiple_of(pair * 384 + part * 128, 128), 128) for part in range(3)]
    for qi in range(length // BLOCK):
        rows = slice(qi * BLOCK, (qi + 1) * BLOCK)
        lo = span(qi, most)
        st = start[:, rows]
        q2 = q_ref[rows, :] * jnp.asarray(0.125, BF16)
        do2 = do_ref[rows, :]
        prod = do2.astype(F32) * o_ref[rows, :].astype(F32)
        high = prod.astype(BF16)
        low = (prod - high.astype(F32)).astype(BF16)
        delta2 = dot_nt(pick, high) + dot_nt(pick, low)
        halves = []
        for h in range(2):
            mine = (lane // 64) == h
            qh = jnp.where(mine, q2, jnp.zeros((), BF16))
            doh = jnp.where(mine, do2, jnp.zeros((), BF16))
            lse = lse_ref[0, h:h + 1, rows]
            delta = delta2[h:h + 1]
            p = jnp.where(pre_seen, jnp.exp(dot_nt(pk, qh) - lse), 0.0)
            ds = (p * (dot_nt(pv, doh) - delta)).astype(BF16)
            one_dpk = dot_nn(ds, qh)
            one_dpv = dot_nn(p.astype(BF16), doh)
            if qi == 0 and h == 0:
                dpk[...], dpv[...] = one_dpk, one_dpv
            else:
                dpk[...] += one_dpk
                dpv[...] += one_dpv
            dq = dot_nn(pk_t[h * 64:(h + 1) * 64], ds)
            for kj in range(lo, qi + 1):
                keys = slice(kj * BLOCK, (kj + 1) * BLOCK)
                s = dot_nt(k_ref[keys, :], qh)
                p = jnp.exp(s - lse)
                p = jnp.where(visible(st, kj * BLOCK, BLOCK, qi * BLOCK, BLOCK, kj == qi), p, 0.0)
                dp = dot_nt(v_ref[keys, :], doh)
                ds = (p * (dp - delta)).astype(BF16)
                dv = dot_nn(p.astype(BF16), doh)
                dk = dot_nn(ds, qh)
                if kj == qi and h == 0:
                    dv_acc[keys, :], dk_acc[keys, :] = dv, dk
                else:
                    dv_acc[keys, :] += dv
                    dk_acc[keys, :] += dk
                dq = dq + dot_nn(k_t[h * 64:(h + 1) * 64, keys], ds)
            halves.append(dq * 0.125)
        gmix[rows, columns[0]] = jnp.concatenate(halves, axis=0).T.astype(BF16)
    gmix[:, columns[1]] = dk_acc[...].astype(BF16)
    gmix[:, columns[2]] = dv_acc[...].astype(BF16)

    def give(part):
        tile = part * pairs + pair
        return pltpu.make_async_remote_copy(
            src_ref=tiles.at[tile], dst_ref=inbox.at[me], send_sem=give_send, recv_sem=give_recv,
            device_id=place(tile * ratio), device_id_type=MESH,
        )

    @pl.when(pair == 0)
    def _():
        pl.semaphore_wait(barrier, devices - 1)

    for part, (ref, half) in enumerate(((dpk, 0), (dpk, 1), (dpv, 0), (dpv, 1))):
        value = ref[half * 8:(half + 1) * 8, :]
        tile = part * pairs + pair
        tiles[pl.ds(tile, 1)] = value[None]
        to_me = owns & (tile == own_tile)

        @pl.when(to_me)
        def _():
            inbox[pl.ds(me, 1)] = value[None]

        @pl.when(jnp.logical_not(to_me))
        def _():
            give(part).start()

    @pl.when(pair == pairs - 1)
    def _():
        for load in loads:
            load.wait()
        tall = 256

        def store(i):
            rows = pl.ds(i * tall, tall)
            return pltpu.make_async_copy(x.at[rows, :], gx_hbm.at[rows, :], out_sems.at[i])

        def finish_rows(i):
            rows = pl.ds(i * tall, tall)
            grad = dot_nt(gmix[rows, :], w[...])
            hat, rate = norm_parts(x[rows, :].astype(F32))
            x[rows, :] = (gm[rows, :] + norm_back(hat, rate, grad, gain_ref[...])).astype(BF16)
            store(i).start()

        def bytes_of(ref, n, send, recv):
            part = ref.at[pl.ds(0, n)]
            return pltpu.make_async_remote_copy(
                src_ref=part, dst_ref=part, send_sem=send, recv_sem=recv,
                device_id=place(lax.rem(me + 1, devices)), device_id_type=MESH,
            )

        finish_rows(0)
        finish_rows(1)

        @pl.when(owns)
        def _():
            bytes_of(inbox, devices - 1, give_send, give_recv).wait_recv()
            summed = inbox[0]
            for device in range(1, devices):
                summed = summed + inbox[device]
            sums[pl.ds(own_tile, 1)] = summed[None]

            @pl.loop(1, devices)
            def _(step):
                pltpu.make_async_remote_copy(
                    src_ref=sums.at[own_tile], dst_ref=sums.at[own_tile], send_sem=tell_send,
                    recv_sem=tell_recv, device_id=place(lax.rem(me + step, devices)), device_id_type=MESH,
                ).start()

        finish_rows(2)
        finish_rows(3)

        @pl.when(owns)
        def _():
            bytes_of(tiles, tile_count - 1, give_send, give_recv).wait_send()
            bytes_of(inbox, devices - 1, tell_send, tell_recv).wait_send()
            bytes_of(tiles, tile_count - 1, tell_send, tell_recv).wait_recv()

        @pl.when(jnp.logical_not(owns))
        def _():
            bytes_of(tiles, tile_count, give_send, give_recv).wait_send()
            bytes_of(tiles, tile_count, tell_send, tell_recv).wait_recv()

        total_ref[...] = sums[...]
        for i in range(length // tall):
            store(i).wait()


def attend_back(dims, mixed, lengths, pre, grad, attended, lse, gain, full_mixer, x, grad_middle, prefix, most):
    length, width = grad.shape
    pairs = width // 128
    count = lengths.shape[1]
    devices = math.prod(dims)
    col = lambda off: pl.BlockSpec((length, 128), lambda p: (0, p + off))
    pcol = lambda off: pl.BlockSpec((PAD, 128), lambda p: (0, p + off))
    anyspace = pl.BlockSpec(memory_space=pl.ANY)
    dma = pltpu.SemaphoreType.DMA
    return pl.pallas_call(
        functools.partial(back_kernel, dims, prefix, most, count),
        grid=(pairs,),
        in_specs=[pl.BlockSpec(memory_space=pltpu.SMEM), pl.BlockSpec((1, length, 384), lambda p: (p, 0, 0)),
                  pcol(0), pcol(pairs), col(0), col(0), pl.BlockSpec((1, 2, length), lambda p: (p, 0, 0)),
                  pl.BlockSpec((1, width), lambda p: (0, 0)), anyspace, anyspace, anyspace],
        out_specs=[anyspace, pl.BlockSpec((4 * pairs, 8, 128), lambda p: (0, 0, 0))],
        out_shape=[jax.ShapeDtypeStruct((length, width), BF16), jax.ShapeDtypeStruct((4 * pairs, 8, 128), F32)],
        scratch_shapes=[pltpu.VMEM((length, 128), F32)] * 2 + [pltpu.VMEM((PAD, 128), F32)] * 2 + [
            pltpu.VMEM((length, 3 * width), BF16), pltpu.VMEM((width, 3 * width), BF16),
            pltpu.VMEM((length, width), BF16), pltpu.VMEM((length, width), F32),
            pltpu.VMEM((4 * pairs, 8, 128), F32), pltpu.VMEM((devices, 8, 128), F32),
            pltpu.VMEM((4 * pairs, 8, 128), F32),
            dma((2 + pairs,)), dma((length // 256,)), dma(()), dma(()), dma(()), dma(()),
        ],
        compiler_params=pltpu.CompilerParams(collective_id=2, has_side_effects=True, vmem_limit_bytes=56 << 20),
        name="attend_back",
    )(lengths, mixed, pre, pre, grad, attended, lse, gain, full_mixer, x, grad_middle)


def reparam_kernel(prefix, total_ref, sq_ref, embed_ref, ro_ref, ri_ref, gx_hbm, out_hbm,
                   gx_out, out_out, ge_ref, gi_ref, gib_ref, go_ref, gob_ref, gs, sems):
    step = pl.program_id(0)
    steps = pl.num_programs(0)
    pairs = total_ref.shape[0] // 4
    moves = [pltpu.make_async_copy(gx_hbm, gx_out, sems.at[0]), pltpu.make_async_copy(out_hbm, out_out, sems.at[1])]

    @pl.when(step == 0)
    def _():
        for move in moves:
            move.start()
        gs[...] = jnp.zeros_like(gs)

    per = 2 * pairs // steps
    blocks = []
    for n in range(per):
        block = step * per + n
        part, pair = block // pairs, lax.rem(block, pairs)
        top = total_ref[pl.ds(2 * part * pairs + pair, 1)][0]
        low = total_ref[pl.ds((2 * part + 1) * pairs + pair, 1)][0]
        blocks.append(jnp.concatenate([top, low], axis=0))
    grad = jnp.concatenate(blocks, axis=1)
    go_ref[...] = dot_fine(sq_ref[...], grad, ((0,), (0,)))
    gob_ref[...] = jnp.sum(grad, axis=0, keepdims=True)
    gs[...] += dot_fine(grad, ro_ref[...], ((1,), (1,)))

    @pl.when(step == steps - 1)
    def _():
        squashed = sq_ref[...]
        inner = gs[...] * (1.0 - squashed * squashed)
        gi_ref[...] = dot_fine(embed_ref[...], inner, ((0,), (0,)))
        gib_ref[...] = jnp.sum(inner, axis=0, keepdims=True)
        ge_ref[...] = dot_fine(inner, ri_ref[...], ((1,), (1,)))[:prefix]
        for move in moves:
            move.wait()


def reparam_back(total, squashed, embed, reparam_out, reparam_in, grad_tokens, out_tokens, prefix):
    width2 = reparam_out.shape[1]
    rep = reparam_out.shape[0]
    width = embed.shape[1]
    steps = 4
    whole = lambda array: pl.BlockSpec(array.shape, lambda i: (0,) * array.ndim)
    anyspace = pl.BlockSpec(memory_space=pl.ANY)
    shape = jax.ShapeDtypeStruct
    return pl.pallas_call(
        functools.partial(reparam_kernel, prefix),
        grid=(steps,),
        in_specs=[whole(total), whole(squashed), whole(embed), pl.BlockSpec((rep, width2 // steps), lambda i: (0, i)),
                  whole(reparam_in), anyspace, anyspace],
        out_specs=[anyspace, anyspace,
                   pl.BlockSpec((prefix, width), lambda i: (0, 0)), pl.BlockSpec((width, rep), lambda i: (0, 0)),
                   pl.BlockSpec((1, rep), lambda i: (0, 0)), pl.BlockSpec((rep, width2 // steps), lambda i: (0, i)),
                   pl.BlockSpec((1, width2 // steps), lambda i: (0, i))],
        out_shape=[shape(grad_tokens.shape, BF16), shape(out_tokens.shape, BF16), shape((prefix, width), F32),
                   shape((width, rep), F32), shape((1, rep), F32), shape((rep, width2), F32), shape((1, width2), F32)],
        scratch_shapes=[pltpu.VMEM(squashed.shape, F32), pltpu.SemaphoreType.DMA((2,))],
        compiler_params=pltpu.CompilerParams(vmem_limit_bytes=40 << 20),
        name="reparam_back",
    )(total, squashed, embed, reparam_out, reparam_in, grad_tokens, out_tokens)


def shards(
    dims,
    tokens,
    lengths,
    cotangent,
    mixer_weight,
    output_weight,
    expand_weight,
    contract_weight,
    mixer_bias,
    output_bias,
    expand_bias,
    contract_bias,
    norm_gains,
    norm_shifts,
    prefix_embed,
    reparam_in,
    reparam_in_bias,
    reparam_out,
    reparam_out_bias,
):
    row_count, length, model_width = tokens.shape
    total_rows = row_count * length
    devices = math.prod(dims)
    hidden = expand_weight.shape[1]
    part = hidden // devices // CHUNKS
    by_chunk = lambda array: array.reshape(-1, devices, CHUNKS, part).transpose(2, 0, 1, 3).reshape(CHUNKS, -1, devices * part)
    expand_parts = by_chunk(expand_weight)
    expand_bias_parts = by_chunk(expand_bias)[:, 0]
    contract_parts = contract_weight.reshape(CHUNKS, part, model_width)
    prefix_count = prefix_embed.shape[0]
    tall = lambda array: jnp.pad(array, ((0, PAD - prefix_count), (0, 0)))
    rows = mixer_weight.shape[0]
    pairs = model_width // 128
    mixer_parts = mixer_weight.reshape(rows, 3, pairs, 128).transpose(2, 0, 1, 3).reshape(pairs, rows, 384)
    x = tokens.reshape(total_rows, model_width)
    as_row = lambda array: array.reshape(1, -1)
    embed = tall(prefix_embed)
    mixed, attended, log_sums, pre, squashed, full_mixer, out_tokens, grad_middle, grad_attended = layer(
        dims, x, lengths, cotangent.reshape(total_rows, model_width), mixer_parts,
        output_weight[None], expand_parts, contract_parts, reparam_in, reparam_out, embed,
        as_row(reparam_in_bias), as_row(reparam_out_bias), as_row(mixer_bias), as_row(output_bias), expand_bias_parts,
        as_row(contract_bias), norm_gains, norm_shifts, prefix_count, MOST,
    )
    grad_tokens, total = attend_back(
        dims, mixed, lengths, pre, grad_attended, attended, log_sums, norm_gains[0:1],
        full_mixer.reshape(pairs, model_width, 384), x, grad_middle, prefix_count, MOST,
    )
    grad_tokens, out_tokens, grad_embed, grad_in, grad_in_bias, grad_out, grad_out_bias = reparam_back(
        total, squashed, embed, reparam_out, reparam_in, grad_tokens, out_tokens, prefix_count
    )
    return (
        out_tokens.reshape(tokens.shape), grad_tokens.reshape(tokens.shape), grad_embed, grad_in, grad_in_bias[0],
        grad_out, grad_out_bias[0],
    )


def solution(mesh):
    return jax.shard_map(
        functools.partial(shards, grid_dims(mesh.shape)),
        mesh=mesh,
        in_specs=(
            P(("wide", "narrow"), None, None),
            P(("wide", "narrow"), None),
            P(("wide", "narrow"), None, None),
            P(("wide", "narrow"), None),
            P(("wide", "narrow"), None),
            P(("wide", "narrow"), None),
            P(("wide", "narrow"), None),
            P(),
            P(),
            P(),
            P(),
            P(),
            P(),
            P(),
            P(),
            P(),
            P(),
            P(),
        ),
        out_specs=(
            P(("wide", "narrow"), None, None),
            P(("wide", "narrow"), None, None),
            P(),
            P(),
            P(),
            P(),
            P(),
        ),
        check_vma=False,
    )
```

```python
import functools
import math

import jax
import jax.numpy as jnp
from jax import lax
from jax.experimental import pallas as pl
from jax.experimental.pallas import tpu as pltpu
from jax.sharding import PartitionSpec as P

MOST = 512


BLOCK = 256
PAD = 16
F32, BF16 = jnp.float32, jnp.bfloat16


def dot_nt(a, b):
    return lax.dot_general(a, b, (((1,), (1,)), ((), ())), preferred_element_type=F32)


def dot_nn(a, b):
    return lax.dot_general(a, b, (((1,), (0,)), ((), ())), preferred_element_type=F32)


def start_row(lengths_ref, count, length):
    place = lax.broadcasted_iota(jnp.int32, (1, length), 1)
    start = jnp.zeros((1, length), jnp.int32)
    total = jnp.int32(0)
    for j in range(count):
        total = total + lengths_ref[0, j]
        start = jnp.where(place >= total, total, start)
    return start


def visible(start, first_key, keys, first_query, queries, diagonal):
    key = lax.broadcasted_iota(jnp.int32, (keys, queries), 0) + first_key
    seen = key >= start
    if diagonal:
        query = lax.broadcasted_iota(jnp.int32, (keys, queries), 1) + first_query
        seen = seen & (key <= query)
    return seen


def span(qi, most):
    return max(0, qi - most // BLOCK)


def fwd_pair(q_ref, k_ref, v_ref, pk, pv, start, prefix, most, o_ref, lse_ref, blocks):
    lane = lax.broadcasted_iota(jnp.int32, (1, 128), 1)
    pre_seen = lax.broadcasted_iota(jnp.int32, (PAD, BLOCK), 0) < prefix
    v_t = v_ref[:(max(blocks) + 1) * BLOCK, :].T
    pv_t = pv.T
    for qi in blocks:
        rows = slice(qi * BLOCK, (qi + 1) * BLOCK)
        lo = span(qi, most)
        st = start[:, rows]
        q2 = q_ref[rows, :] * jnp.asarray(0.125, BF16)
        halves = []
        for h in range(2):
            qh = jnp.where((lane // 64) == h, q2, jnp.zeros((), BF16))
            s_pre = jnp.where(pre_seen, dot_nt(pk, qh), -1e30)
            peak = jnp.max(s_pre, axis=0, keepdims=True)
            parts = []
            for kj in range(lo, qi + 1):
                s = dot_nt(k_ref[kj * BLOCK:(kj + 1) * BLOCK, :], qh)
                s = jnp.where(visible(st, kj * BLOCK, BLOCK, qi * BLOCK, BLOCK, kj == qi), s, -1e30)
                peak = jnp.maximum(peak, jnp.max(s, axis=0, keepdims=True))
                parts.append(s)
            p = jnp.exp(s_pre - peak)
            total = jnp.sum(p, axis=0, keepdims=True)
            o = dot_nn(pv_t[h * 64:(h + 1) * 64], p.astype(BF16))
            for n, kj in enumerate(range(lo, qi + 1)):
                p = jnp.exp(parts[n] - peak)
                total = total + jnp.sum(p, axis=0, keepdims=True)
                o = o + dot_nn(v_t[h * 64:(h + 1) * 64, kj * BLOCK:(kj + 1) * BLOCK], p.astype(BF16))
            halves.append(o / total)
            lse_ref[h:h + 1, rows] = peak + jnp.log(total)
        o_ref[rows, :] = jnp.concatenate(halves, axis=0).T.astype(BF16)


CHUNKS = 8
TILE = 256
MESH = pl.DeviceIdType.MESH
XY, YX = (0, 1, 2, 3), (0, 2, 1, 3)


def grid_dims(mesh_shape):
    wide, narrow = mesh_shape["wide"], mesh_shape["narrow"]
    return (wide // 2, 2, narrow // 2, 2)


class Family:
    def __init__(self, source, target, order, sems, part=()):
        self.source, self.target, self.order, self.part = source, target, order, part
        self.send, self.recv, self.own = sems


class Group:
    def __init__(self, families, offset, lag, ahead):
        self.families, self.offset, self.lag, self.ahead = families, offset, lag, ahead
        self.count = families[0].source.shape[0]

    def tick(self, stage):
        return self.offset + (self.lag * stage if stage >= 0 else -self.ahead)


class Gather:
    def __init__(self, dims, groups):
        self.dims = dims
        wide, narrow = lax.axis_index("wide"), lax.axis_index("narrow")
        self.at = (wide // dims[1], lax.rem(wide, dims[1]), narrow // dims[3], lax.rem(narrow, dims[3]))
        self.groups = groups
        self.peers = [
            [self.device(dim, lax.rem(self.at[dim] + step, size)) for step in range(1, size)]
            for dim, size in enumerate(dims)
        ]

    def device(self, dim, index):
        at = list(self.at)
        at[dim] = index
        return (at[0] * self.dims[1] + at[1], at[2] * self.dims[3] + at[3])

    def greet(self):
        barrier = pltpu.get_barrier_semaphore()
        for peers in self.peers:
            for peer in peers:
                pl.semaphore_signal(barrier, inc=1, device_id=peer, device_id_type=MESH)
        pl.semaphore_wait(barrier, sum(len(peers) for peers in self.peers))

    def view(self, family, j, stage, index):
        done, dim = family.order[:stage], family.order[stage]
        return family.target.at[
            (j,)
            + tuple(slice(None) if d in done else (index if d == dim else self.at[d]) for d in range(4))
            + family.part
        ]

    def keep(self, family, j):
        return pltpu.make_async_copy(
            family.source.at[(j,) + family.part], family.target.at[(j,) + self.at + family.part], family.own.at[j]
        )

    def start(self, family, j, stage):
        dim = family.order[stage]
        if stage == 0:
            self.keep(family, j).start()
        mine = self.view(family, j, stage, self.at[dim])
        for peer in self.peers[dim]:
            pltpu.make_async_remote_copy(
                src_ref=family.source.at[(j,) + family.part] if stage == 0 else mine,
                dst_ref=mine,
                send_sem=family.send.at[j, stage],
                recv_sem=family.recv.at[j, stage],
                device_id=peer,
                device_id_type=MESH,
            ).start()

    def whole(self, family, j, stage):
        dim = family.order[stage]
        part = self.view(family, j, stage, pl.ds(0, self.dims[dim] - 1))
        return pltpu.make_async_remote_copy(
            src_ref=part, dst_ref=part, send_sem=family.send.at[j, stage], recv_sem=family.recv.at[j, stage],
            device_id=self.peers[dim][0], device_id_type=MESH,
        )

    def arrive(self, family, j, stage):
        if stage == 0:
            self.keep(family, j).wait()
        self.whole(family, j, stage).wait_recv()

    def begin(self):
        for group in self.groups:
            for j in range(group.count):
                if group.tick(-1) + 2 * j < 0:
                    for family in group.families:
                        self.start(family, j, 0)

    def tick(self, double, half):
        for stage in (3, 2, 1, 0, -1):
            for group in self.groups:
                past = half - group.tick(stage)
                if past % 2:
                    continue
                j = double + past // 2

                @pl.when((j >= 0) & (j < group.count))
                def _():
                    for family in group.families:
                        if stage >= 0:
                            self.arrive(family, j, stage)
                        if stage < 3:
                            self.start(family, j, stage + 1)

    def finish(self):
        for group in self.groups:

            @pl.loop(0, group.count)
            def _(j):
                for family in group.families:
                    for stage in range(4):
                        self.whole(family, j, stage).wait_send()


def gather_sems(count):
    dma = pltpu.SemaphoreType.DMA
    return [dma((count, 4)), dma((count, 4)), dma((count,))]


def norm_parts(values):
    center = values - jnp.mean(values, axis=-1, keepdims=True)
    rate = lax.rsqrt(jnp.mean(center * center, axis=-1, keepdims=True) + 1e-05)
    return center * rate, rate


def norm_back(hat, rate, grad, gain):
    inner = grad * gain
    return rate * (
        inner - jnp.mean(inner, axis=-1, keepdims=True) - hat * jnp.mean(inner * hat, axis=-1, keepdims=True)
    )


def split(value):
    high = value.astype(BF16)
    return high, (value - high.astype(F32)).astype(BF16)


def dot_fine(left, right, dims):
    lh, ll = split(left)
    rh, rl = split(right)
    one = lambda a, b: lax.dot_general(a, b, (dims, ((), ())), preferred_element_type=F32)
    return one(lh, rh) + (one(lh, rl) + one(ll, rh))


ROOT = math.sqrt(2.0 / math.pi)


def gelu_both(v):
    square = v * v
    th = jnp.tanh(ROOT * v * (1.0 + 0.044715 * square))
    half = 0.5 * (1.0 + th)
    slope = half + 0.5 * v * (1.0 - th * th) * (ROOT * (1.0 + 3 * 0.044715 * square))
    return v * half, slope


M_LAG = 3
PAIR_TICK = 9
MID_TICK = 25
FF_TICK = 27
FF_LAG = 3
W_TICK = 12
AHEAD = 7


def layer_kernel(dims, prefix, most, count, len_ref, x_hbm, cot_hbm, m_hbm, w_hbm, e_hbm, c_hbm, ri_hbm, ro_hbm,
                 embed_ref, rib_ref, rob_ref, mb_ref, bo_ref, be_ref, bc_ref, gain_ref, shift_ref,
                 mixed_hbm, att_hbm, lse_ref, pre_ref, sq_ref, mixer_hbm, out_hbm, gm_hbm, ga_hbm,
                 x, norm, mixer, mixed, att, cot, wo, mid, acc, gacc, ew, cw,
                 m0_send, m0_recv, m0_own, m1_send, m1_recv, m1_own, w0_send, w0_recv, w0_own, w1_send, w1_recv, w1_own,
                 e_send, e_recv, e_own, c_send, c_recv, c_own,
                 in_sems, mixed_sems, att_sems, mixer_sems, out_sems):
    length, width = x.shape
    pairs, chunks = m_hbm.shape[0], e_hbm.shape[0]
    rep = sq_ref.shape[1]
    both = lambda rows: [(order, (pl.ds(n * rows // 2, rows // 2),)) for n, order in enumerate((XY, YX))]
    m_sems = ((m0_send, m0_recv, m0_own), (m1_send, m1_recv, m1_own))
    w_sems = ((w0_send, w0_recv, w0_own), (w1_send, w1_recv, w1_own))
    halves = lambda rows: [(order, (pl.ds(n * rows // 2, rows // 2),)) for n, order in enumerate((XY, YX))]
    m_sems = ((m0_send, m0_recv, m0_own), (m1_send, m1_recv, m1_own))
    w_sems = ((w0_send, w0_recv, w0_own), (w1_send, w1_recv, w1_own))
    gather = Gather(dims, [
        Group([Family(m_hbm, mixer, order, m_sems[n], part) for n, (order, part) in enumerate(halves(m_hbm.shape[1]))],
              0, M_LAG, AHEAD),
        Group([Family(w_hbm, wo, order, w_sems[n], part) for n, (order, part) in enumerate(halves(w_hbm.shape[1]))],
              W_TICK, 2, AHEAD),
        Group([Family(e_hbm, ew, XY, (e_send, e_recv, e_own)), Family(c_hbm, cw, YX, (c_send, c_recv, c_own))],
              FF_TICK - 3 * FF_LAG, FF_LAG, AHEAD),
    ])
    loads = [
        pltpu.make_async_copy(src, dst, in_sems.at[n])
        for n, (src, dst) in enumerate((
            (x_hbm, x), (ri_hbm, mid.at[:, :rep]), (ro_hbm.at[:, :width], acc.at[:rep]), (ro_hbm.at[:, width:], gacc.at[:rep]),
            (cot_hbm, cot),
        ))
    ]
    for load in loads:
        load.start()
    gather.greet()
    gather.begin()
    tiles = length // TILE

    def rows_of(i):
        return pl.ds(pl.multiple_of(i * TILE, TILE), TILE)

    def first_norm():
        loads[0].wait()

        @pl.loop(0, tiles)
        def _(i):
            rows = rows_of(i)
            hat, _ = norm_parts(x[rows, :].astype(F32))
            norm[rows, :] = (hat * gain_ref[0:1, :] + shift_ref[0:1, :]).astype(BF16)

    def prefix_rows():
        for load in loads[1:]:
            load.wait()
        seen = lax.broadcasted_iota(jnp.int32, (PAD, 1), 0) < prefix
        squashed = jnp.where(seen, jnp.tanh(dot_fine(embed_ref[...], mid[:, :rep], ((1,), (0,))) + rib_ref[...]), 0.0)
        sq_ref[...] = squashed
        for part, ref in enumerate((acc, gacc)):
            columns = slice(part * width, (part + 1) * width)
            whole = dot_fine(squashed, ref[:rep, :], ((1,), (0,))) + rob_ref[:, columns]
            pre_ref[:, columns] = jnp.where(seen, whole, 0.0).astype(BF16)

    def stores(p, slot):
        columns = pl.ds(pl.multiple_of(p * 128, 128), 128)
        return [
            pltpu.make_async_copy(mixed.at[slot], mixed_hbm.at[p], mixed_sems.at[slot]),
            pltpu.make_async_copy(att.at[:, columns], att_hbm.at[:, columns], att_sems.at[slot]),
        ]

    def keep_mixer(p):
        return pltpu.make_async_copy(mixer.at[p], mixer_hbm.at[p], mixer_sems.at[p])

    def pair(p, part):
        slot = lax.rem(p, 2)
        at = [pl.ds(pl.multiple_of(third * width + p * 128, 128), 128) for third in range(3)]
        here = mixed.at[slot]

        if part == 0:

            @pl.when(p >= 2)
            def _():
                for store in stores(p - 2, slot):
                    store.wait()

            keep_mixer(p).start()
            weight = mixer[pl.ds(p, 1)].reshape(width, 384)
            bias = jnp.concatenate([mb_ref[:, columns] for columns in at], axis=1)
            mixed[pl.ds(slot, 1)] = (dot_nn(norm[...], weight) + bias).astype(BF16)[None]
        blocks = length // BLOCK
        fwd_pair(
            here.at[:, 0:128], here.at[:, 128:256], here.at[:, 256:384], pre_ref[:, at[0]], pre_ref[:, at[1]],
            start_row(len_ref, count, length), prefix, most, att.at[:, at[0]], lse_ref.at[p],
            range(blocks // 2) if part == 0 else range(blocks // 2, blocks),
        )
        if part == 1:
            for store in stores(p, slot):
                store.start()

    def output_weight():
        return wo[0].reshape(width, width)

    def second_norm(part):
        if part == 0:
            for p in (pairs - 2, pairs - 1):
                for store in stores(p, p % 2):
                    store.wait()

        @pl.loop(part * tiles // 2, (part + 1) * tiles // 2)
        def _(i):
            rows = rows_of(i)
            value = x[rows, :].astype(F32) + (dot_nn(att[rows, :], output_weight()) + bo_ref[...])
            mid[rows, :] = value
            hat, _ = norm_parts(value)
            norm[rows, :] = (hat * gain_ref[1:2, :] + shift_ref[1:2, :]).astype(BF16)
            acc[rows, :] = jnp.zeros((TILE, width), F32)
            gacc[rows, :] = jnp.zeros((TILE, width), F32)

    def chunk(j, part):
        e = ew.at[j]
        c = cw.at[j]
        bias = be_ref[pl.ds(j, 1), :]

        @pl.loop(part * tiles // 2, (part + 1) * tiles // 2)
        def _(i):
            rows = rows_of(i)
            ev = e[...].reshape(width, -1)
            cv = c[...].reshape(-1, width)
            active, slope = gelu_both(dot_nn(norm[rows, :], ev) + bias)
            grad = (dot_nt(cot[rows, :], cv) * slope).astype(BF16)
            acc[rows, :] += dot_nn(active.astype(BF16), cv)
            gacc[rows, :] += dot_nt(grad, ev)

    @pl.loop(0, (FF_TICK + 2 * chunks + 1) // 2)
    def _(double):
        for half in range(2):
            gather.tick(double, half)
            if half == 0:
                pl.when(double == 0)(first_norm)
            else:
                pl.when(double == 0)(prefix_rows)
            part = (half - PAIR_TICK) % 2
            p = double + (half - PAIR_TICK) // 2

            @pl.when((p >= 0) & (p < pairs))
            def _():
                pair(p, part)

            part = (half - MID_TICK) % 2
            pl.when(double + (half - MID_TICK) // 2 == 0)(functools.partial(second_norm, part))
            part = (half - FF_TICK) % 2
            j = double + (half - FF_TICK) // 2

            @pl.when((j >= 0) & (j < chunks))
            def _():
                chunk(j, part)

    def results(i):
        rows = rows_of(i)
        return [
            pltpu.make_async_copy(src.at[rows, :], dst.at[rows, :], out_sems.at[n, i])
            for n, (src, dst) in enumerate(((x, out_hbm), (gacc, gm_hbm), (att, ga_hbm)))
        ]

    @pl.loop(0, tiles)
    def _(i):
        rows = rows_of(i)
        value = mid[rows, :]
        x[rows, :] = (value + (acc[rows, :] + bc_ref[...])).astype(BF16)
        hat, rate = norm_parts(value)
        grad = cot[rows, :].astype(F32) + norm_back(hat, rate, gacc[rows, :], gain_ref[1:2, :])
        gacc[rows, :] = grad
        att[rows, :] = dot_nt(grad.astype(BF16), output_weight()).astype(BF16)
        for result in results(i):
            result.start()

    gather.finish()

    @pl.loop(0, pairs)
    def _(p):
        keep_mixer(p).wait()

    @pl.loop(0, tiles)
    def _(i):
        for result in results(i):
            result.wait()


def layer(dims, x, lengths, cot, m_shard, w_shard, e_shard, c_shard, reparam_in, reparam_out, embed, reparam_in_bias,
          reparam_out_bias, mixer_bias, output_bias, expand_bias, contract_bias, gains, shifts, prefix, most):
    length, width = x.shape
    pairs, chunks = m_shard.shape[0], e_shard.shape[0]
    rep = reparam_in.shape[1]
    anyspace = pl.BlockSpec(memory_space=pl.ANY)
    vmem = pl.BlockSpec(memory_space=pltpu.VMEM)
    dma = pltpu.SemaphoreType.DMA
    shape = jax.ShapeDtypeStruct
    held = lambda shard: (shard.shape[0],) + dims + shard.shape[1:]
    full = lambda kind: pltpu.VMEM((length, width), kind)
    return pl.pallas_call(
        functools.partial(layer_kernel, dims, prefix, most, lengths.shape[1]),
        in_specs=[pl.BlockSpec(memory_space=pltpu.SMEM)] + [anyspace] * 8 + [vmem] * 9,
        out_specs=[anyspace, anyspace, vmem, vmem, vmem] + [anyspace] * 4,
        out_shape=[
            shape((pairs, length, 384), BF16), shape((length, width), BF16), shape((pairs, 2, length), F32),
            shape((PAD, 2 * width), BF16), shape((PAD, rep), F32), shape(held(m_shard), BF16),
            shape((length, width), BF16), shape((length, width), F32), shape((length, width), BF16),
        ],
        scratch_shapes=[
            full(BF16), full(BF16), pltpu.VMEM(held(m_shard), BF16), pltpu.VMEM((2, length, 384), BF16), full(BF16),
            full(BF16), pltpu.VMEM(held(w_shard), BF16), full(F32), full(F32), full(F32),
            pltpu.VMEM(held(e_shard), BF16), pltpu.VMEM(held(c_shard), BF16),
            *gather_sems(pairs), *gather_sems(pairs), *gather_sems(1), *gather_sems(1),
            *gather_sems(chunks), *gather_sems(chunks),
            dma((5,)), dma((2,)), dma((2,)), dma((pairs,)), dma((3, length // TILE)),
        ],
        compiler_params=pltpu.CompilerParams(collective_id=0, has_side_effects=True, vmem_limit_bytes=60 << 20),
        name="layer",
    )(lengths, x, cot, m_shard, w_shard, e_shard, c_shard, reparam_in, reparam_out, embed, reparam_in_bias,
      reparam_out_bias, mixer_bias, output_bias, expand_bias, contract_bias, gains, shifts)


def back_kernel(dims, prefix, most, count, len_ref, mixed_ref, pk_ref, pv_ref, do_ref, o_ref, lse_ref,
                gain_ref, w_hbm, x_hbm, gm_hbm, gx_hbm, total_ref,
                dk_acc, dv_acc, dpk, dpv, gmix, w, x, gm, tiles, inbox, sums,
                in_sems, out_sems, give_send, give_recv, tell_send, tell_recv):
    length, width = x.shape
    q_ref, k_ref, v_ref = (mixed_ref.at[0, :, part * 128:(part + 1) * 128] for part in range(3))
    pair = pl.program_id(0)
    pairs = width // 128
    devices = math.prod(dims)
    narrow_size = dims[2] * dims[3]
    me = lax.axis_index("wide") * narrow_size + lax.axis_index("narrow")
    tile_count = 4 * pairs
    ratio = devices // tile_count
    owns = lax.rem(me, ratio) == 0
    own_tile = me // ratio
    place = lambda device: (device // narrow_size, lax.rem(device, narrow_size))
    loads = [
        pltpu.make_async_copy(src, dst, in_sems.at[n])
        for n, (src, dst) in enumerate(((x_hbm, x), (gm_hbm, gm)))
    ] + [
        pltpu.make_async_copy(w_hbm.at[n], w.at[:, n * 384:(n + 1) * 384], in_sems.at[2 + n]) for n in range(pairs)
    ]
    barrier = pltpu.get_barrier_semaphore()

    @pl.when(pair == 0)
    def _():
        for load in loads:
            load.start()

        @pl.loop(1, devices)
        def _(step):
            peer = place(lax.rem(me + step, devices))
            pl.semaphore_signal(barrier, inc=1, device_id=peer, device_id_type=MESH)

    start = start_row(len_ref, count, length)
    lane = lax.broadcasted_iota(jnp.int32, (1, 128), 1)
    pre_seen = lax.broadcasted_iota(jnp.int32, (PAD, BLOCK), 0) < prefix
    pk, pv = pk_ref[...], pv_ref[...]
    k_t = k_ref[...].T
    pk_t = pk.T
    head_of = lax.broadcasted_iota(jnp.int32, (8, 128), 0)
    pick = ((lax.broadcasted_iota(jnp.int32, (8, 128), 1) // 64) == head_of).astype(F32).astype(BF16)
    columns = [pl.ds(pl.multiple_of(pair * 384 + part * 128, 128), 128) for part in range(3)]
    for qi in range(length // BLOCK):
        rows = slice(qi * BLOCK, (qi + 1) * BLOCK)
        lo = span(qi, most)
        st = start[:, rows]
        q2 = q_ref[rows, :] * jnp.asarray(0.125, BF16)
        do2 = do_ref[rows, :]
        prod = do2.astype(F32) * o_ref[rows, :].astype(F32)
        high = prod.astype(BF16)
        low = (prod - high.astype(F32)).astype(BF16)
        delta2 = dot_nt(pick, high) + dot_nt(pick, low)
        halves = []
        for h in range(2):
            mine = (lane // 64) == h
            qh = jnp.where(mine, q2, jnp.zeros((), BF16))
            doh = jnp.where(mine, do2, jnp.zeros((), BF16))
            lse = lse_ref[0, h:h + 1, rows]
            delta = delta2[h:h + 1]
            p = jnp.where(pre_seen, jnp.exp(dot_nt(pk, qh) - lse), 0.0)
            ds = (p * (dot_nt(pv, doh) - delta)).astype(BF16)
            one_dpk = dot_nn(ds, qh)
            one_dpv = dot_nn(p.astype(BF16), doh)
            if qi == 0 and h == 0:
                dpk[...], dpv[...] = one_dpk, one_dpv
            else:
                dpk[...] += one_dpk
                dpv[...] += one_dpv
            dq = dot_nn(pk_t[h * 64:(h + 1) * 64], ds)
            for kj in range(lo, qi + 1):
                keys = slice(kj * BLOCK, (kj + 1) * BLOCK)
                s = dot_nt(k_ref[keys, :], qh)
                p = jnp.exp(s - lse)
                p = jnp.where(visible(st, kj * BLOCK, BLOCK, qi * BLOCK, BLOCK, kj == qi), p, 0.0)
                dp = dot_nt(v_ref[keys, :], doh)
                ds = (p * (dp - delta)).astype(BF16)
                dv = dot_nn(p.astype(BF16), doh)
                dk = dot_nn(ds, qh)
                if kj == qi and h == 0:
                    dv_acc[keys, :], dk_acc[keys, :] = dv, dk
                else:
                    dv_acc[keys, :] += dv
                    dk_acc[keys, :] += dk
                dq = dq + dot_nn(k_t[h * 64:(h + 1) * 64, keys], ds)
            halves.append(dq * 0.125)
        gmix[rows, columns[0]] = jnp.concatenate(halves, axis=0).T.astype(BF16)
    gmix[:, columns[1]] = dk_acc[...].astype(BF16)
    gmix[:, columns[2]] = dv_acc[...].astype(BF16)

    def give(part):
        tile = part * pairs + pair
        return pltpu.make_async_remote_copy(
            src_ref=tiles.at[tile], dst_ref=inbox.at[me], send_sem=give_send, recv_sem=give_recv,
            device_id=place(tile * ratio), device_id_type=MESH,
        )

    @pl.when(pair == 0)
    def _():
        pl.semaphore_wait(barrier, devices - 1)

    for part, (ref, half) in enumerate(((dpk, 0), (dpk, 1), (dpv, 0), (dpv, 1))):
        value = ref[half * 8:(half + 1) * 8, :]
        tile = part * pairs + pair
        tiles[pl.ds(tile, 1)] = value[None]
        to_me = owns & (tile == own_tile)

        @pl.when(to_me)
        def _():
            inbox[pl.ds(me, 1)] = value[None]

        @pl.when(jnp.logical_not(to_me))
        def _():
            give(part).start()

    @pl.when(pair == pairs - 1)
    def _():
        for load in loads:
            load.wait()
        tall = 256

        def store(i):
            rows = pl.ds(i * tall, tall)
            return pltpu.make_async_copy(x.at[rows, :], gx_hbm.at[rows, :], out_sems.at[i])

        def finish_rows(i):
            rows = pl.ds(i * tall, tall)
            grad = dot_nt(gmix[rows, :], w[...])
            hat, rate = norm_parts(x[rows, :].astype(F32))
            x[rows, :] = (gm[rows, :] + norm_back(hat, rate, grad, gain_ref[0:1, :])).astype(BF16)
            store(i).start()

        def bytes_of(ref, n, send, recv):
            part = ref.at[pl.ds(0, n)]
            return pltpu.make_async_remote_copy(
                src_ref=part, dst_ref=part, send_sem=send, recv_sem=recv,
                device_id=place(lax.rem(me + 1, devices)), device_id_type=MESH,
            )

        finish_rows(0)
        finish_rows(1)

        @pl.when(owns)
        def _():
            bytes_of(inbox, devices - 1, give_send, give_recv).wait_recv()
            summed = inbox[0]
            for device in range(1, devices):
                summed = summed + inbox[device]
            sums[pl.ds(own_tile, 1)] = summed[None]

            @pl.loop(1, devices)
            def _(step):
                pltpu.make_async_remote_copy(
                    src_ref=sums.at[own_tile], dst_ref=sums.at[own_tile], send_sem=tell_send,
                    recv_sem=tell_recv, device_id=place(lax.rem(me + step, devices)), device_id_type=MESH,
                ).start()

        finish_rows(2)
        finish_rows(3)

        @pl.when(owns)
        def _():
            bytes_of(tiles, tile_count - 1, give_send, give_recv).wait_send()
            bytes_of(inbox, devices - 1, tell_send, tell_recv).wait_send()
            bytes_of(tiles, tile_count - 1, tell_send, tell_recv).wait_recv()

        @pl.when(jnp.logical_not(owns))
        def _():
            bytes_of(tiles, tile_count, give_send, give_recv).wait_send()
            bytes_of(tiles, tile_count, tell_send, tell_recv).wait_recv()

        total_ref[...] = sums[...]
        for i in range(length // tall):
            store(i).wait()


def attend_back(dims, mixed, lengths, pre, grad, attended, lse, gain, full_mixer, x, grad_middle, prefix, most):
    length, width = grad.shape
    pairs = width // 128
    count = lengths.shape[1]
    devices = math.prod(dims)
    col = lambda off: pl.BlockSpec((length, 128), lambda p: (0, p + off))
    pcol = lambda off: pl.BlockSpec((PAD, 128), lambda p: (0, p + off))
    anyspace = pl.BlockSpec(memory_space=pl.ANY)
    dma = pltpu.SemaphoreType.DMA
    return pl.pallas_call(
        functools.partial(back_kernel, dims, prefix, most, count),
        grid=(pairs,),
        in_specs=[pl.BlockSpec(memory_space=pltpu.SMEM), pl.BlockSpec((1, length, 384), lambda p: (p, 0, 0)),
                  pcol(0), pcol(pairs), col(0), col(0), pl.BlockSpec((1, 2, length), lambda p: (p, 0, 0)),
                  pl.BlockSpec((2, width), lambda p: (0, 0)), anyspace, anyspace, anyspace],
        out_specs=[anyspace, pl.BlockSpec((4 * pairs, 8, 128), lambda p: (0, 0, 0))],
        out_shape=[jax.ShapeDtypeStruct((length, width), BF16), jax.ShapeDtypeStruct((4 * pairs, 8, 128), F32)],
        scratch_shapes=[pltpu.VMEM((length, 128), F32)] * 2 + [pltpu.VMEM((PAD, 128), F32)] * 2 + [
            pltpu.VMEM((length, 3 * width), BF16), pltpu.VMEM((width, 3 * width), BF16),
            pltpu.VMEM((length, width), BF16), pltpu.VMEM((length, width), F32),
            pltpu.VMEM((4 * pairs, 8, 128), F32), pltpu.VMEM((devices, 8, 128), F32),
            pltpu.VMEM((4 * pairs, 8, 128), F32),
            dma((2 + pairs,)), dma((length // 256,)), dma(()), dma(()), dma(()), dma(()),
        ],
        compiler_params=pltpu.CompilerParams(collective_id=2, has_side_effects=True, vmem_limit_bytes=56 << 20),
        name="attend_back",
    )(lengths, mixed, pre, pre, grad, attended, lse, gain, full_mixer, x, grad_middle)


def reparam_kernel(prefix, total_ref, sq_ref, embed_ref, ro_ref, ri_ref, gx_hbm, out_hbm,
                   gx_out, out_out, ge_ref, gi_ref, gib_ref, go_ref, gob_ref, gs, sems):
    step = pl.program_id(0)
    steps = pl.num_programs(0)
    pairs = total_ref.shape[0] // 4
    moves = [pltpu.make_async_copy(gx_hbm, gx_out, sems.at[0]), pltpu.make_async_copy(out_hbm, out_out, sems.at[1])]

    @pl.when(step == 0)
    def _():
        for move in moves:
            move.start()
        gs[...] = jnp.zeros_like(gs)

    per = 2 * pairs // steps
    blocks = []
    for n in range(per):
        block = step * per + n
        part, pair = block // pairs, lax.rem(block, pairs)
        top = total_ref[pl.ds(2 * part * pairs + pair, 1)][0]
        low = total_ref[pl.ds((2 * part + 1) * pairs + pair, 1)][0]
        blocks.append(jnp.concatenate([top, low], axis=0))
    grad = jnp.concatenate(blocks, axis=1)
    go_ref[...] = dot_fine(sq_ref[...], grad, ((0,), (0,)))
    gob_ref[...] = jnp.sum(grad, axis=0, keepdims=True)
    gs[...] += dot_fine(grad, ro_ref[...], ((1,), (1,)))

    @pl.when(step == steps - 1)
    def _():
        squashed = sq_ref[...]
        inner = gs[...] * (1.0 - squashed * squashed)
        gi_ref[...] = dot_fine(embed_ref[...], inner, ((0,), (0,)))
        gib_ref[...] = jnp.sum(inner, axis=0, keepdims=True)
        ge_ref[...] = dot_fine(inner, ri_ref[...], ((1,), (1,)))[:prefix]
        for move in moves:
            move.wait()


def reparam_back(total, squashed, embed, reparam_out, reparam_in, grad_tokens, out_tokens, prefix):
    width2 = reparam_out.shape[1]
    rep = reparam_out.shape[0]
    width = embed.shape[1]
    steps = 4
    whole = lambda array: pl.BlockSpec(array.shape, lambda i: (0,) * array.ndim)
    anyspace = pl.BlockSpec(memory_space=pl.ANY)
    shape = jax.ShapeDtypeStruct
    return pl.pallas_call(
        functools.partial(reparam_kernel, prefix),
        grid=(steps,),
        in_specs=[whole(total), whole(squashed), whole(embed), pl.BlockSpec((rep, width2 // steps), lambda i: (0, i)),
                  whole(reparam_in), anyspace, anyspace],
        out_specs=[anyspace, anyspace,
                   pl.BlockSpec((prefix, width), lambda i: (0, 0)), pl.BlockSpec((width, rep), lambda i: (0, 0)),
                   pl.BlockSpec((1, rep), lambda i: (0, 0)), pl.BlockSpec((rep, width2 // steps), lambda i: (0, i)),
                   pl.BlockSpec((1, width2 // steps), lambda i: (0, i))],
        out_shape=[shape(grad_tokens.shape, BF16), shape(out_tokens.shape, BF16), shape((prefix, width), F32),
                   shape((width, rep), F32), shape((1, rep), F32), shape((rep, width2), F32), shape((1, width2), F32)],
        scratch_shapes=[pltpu.VMEM(squashed.shape, F32), pltpu.SemaphoreType.DMA((2,))],
        compiler_params=pltpu.CompilerParams(vmem_limit_bytes=40 << 20),
        name="reparam_back",
    )(total, squashed, embed, reparam_out, reparam_in, grad_tokens, out_tokens)


def shards(
    dims,
    tokens,
    lengths,
    cotangent,
    mixer_weight,
    output_weight,
    expand_weight,
    contract_weight,
    mixer_bias,
    output_bias,
    expand_bias,
    contract_bias,
    norm_gains,
    norm_shifts,
    prefix_embed,
    reparam_in,
    reparam_in_bias,
    reparam_out,
    reparam_out_bias,
):
    row_count, length, model_width = tokens.shape
    total_rows = row_count * length
    devices = math.prod(dims)
    hidden = expand_weight.shape[1]
    part = hidden // devices // CHUNKS
    by_chunk = lambda array: array.reshape(-1, devices, CHUNKS, part).transpose(2, 0, 1, 3).reshape(CHUNKS, -1, devices * part)
    expand_parts = by_chunk(expand_weight)
    expand_bias_parts = by_chunk(expand_bias)[:, 0]
    contract_parts = contract_weight.reshape(CHUNKS, part, model_width)
    prefix_count = prefix_embed.shape[0]
    tall = lambda array: jnp.pad(array, ((0, PAD - prefix_count), (0, 0)))
    rows = mixer_weight.shape[0]
    pairs = model_width // 128
    mixer_parts = mixer_weight.reshape(rows, 3, pairs, 128).transpose(2, 0, 1, 3).reshape(pairs, rows, 384)
    x = tokens.reshape(total_rows, model_width)
    as_row = lambda array: array.reshape(1, -1)
    embed = tall(prefix_embed)
    mixed, attended, log_sums, pre, squashed, full_mixer, out_tokens, grad_middle, grad_attended = layer(
        dims, x, lengths, cotangent.reshape(total_rows, model_width), mixer_parts,
        output_weight[None], expand_parts, contract_parts, reparam_in, reparam_out, embed,
        as_row(reparam_in_bias), as_row(reparam_out_bias), as_row(mixer_bias), as_row(output_bias), expand_bias_parts,
        as_row(contract_bias), norm_gains, norm_shifts, prefix_count, MOST,
    )
    grad_tokens, total = attend_back(
        dims, mixed, lengths, pre, grad_attended, attended, log_sums, norm_gains,
        full_mixer.reshape(pairs, model_width, 384), x, grad_middle, prefix_count, MOST,
    )
    grad_tokens, out_tokens, grad_embed, grad_in, grad_in_bias, grad_out, grad_out_bias = reparam_back(
        total, squashed, embed, reparam_out, reparam_in, grad_tokens, out_tokens, prefix_count
    )
    return (
        out_tokens.reshape(tokens.shape), grad_tokens.reshape(tokens.shape), grad_embed, grad_in, grad_in_bias[0],
        grad_out, grad_out_bias[0],
    )


def solution(mesh):
    return jax.shard_map(
        functools.partial(shards, grid_dims(mesh.shape)),
        mesh=mesh,
        in_specs=(
            P(("wide", "narrow"), None, None),
            P(("wide", "narrow"), None),
            P(("wide", "narrow"), None, None),
            P(("wide", "narrow"), None),
            P(("wide", "narrow"), None),
            P(("wide", "narrow"), None),
            P(("wide", "narrow"), None),
            P(),
            P(),
            P(),
            P(),
            P(),
            P(),
            P(),
            P(),
            P(),
            P(),
            P(),
        ),
        out_specs=(
            P(("wide", "narrow"), None, None),
            P(("wide", "narrow"), None, None),
            P(),
            P(),
            P(),
            P(),
            P(),
        ),
        check_vma=False,
    )
```
